32 devices in a mesh: ctx: 8 (over z, x), tp: 4 (over y, core).
Axes of the slice: x: 2, y: 2, z: 4, core: 2. Of those that a mesh axis runs over, the one named last changes fastest.
Arguments:
- queries: bfloat16 [8192, 1024], P('tp', 'ctx'), may hold values from -6 to 6
- key_signal: bfloat16 [8192, 1024], P('tp', 'ctx'), may hold values from -6 to 6
- value_signal: bfloat16 [8192, 1024], P('tp', 'ctx'), may hold values from -6 to 6
- cotangent: bfloat16 [8192, 1024], P('tp', 'ctx'), may hold values from -6 to 6
- short_weight: float32 [3, 7, 8192], P(None, None, 'tp'), may hold values from -2 to 2
- residues: float32 [8192, 16], P('tp'), may hold values from -1.5 to 1.5
- decay_rates: float32 [8192, 16], P('tp'), may hold values from 0.0001 to 0.03
- skip_gain: float32 [8192], P('tp'), may hold values from 0.5 to 1.5
Outputs:
- mixed: bfloat16 [8192, 1024], P('tp', 'ctx')
- grad_queries: bfloat16 [8192, 1024], P('tp', 'ctx')
- grad_keys: bfloat16 [8192, 1024], P('tp', 'ctx')
- grad_values: bfloat16 [8192, 1024], P('tp', 'ctx')
- grad_short: float32 [3, 7, 8192], P(None, None, 'tp')
- grad_residues: float32 [8192, 16], P('tp')
- grad_skip: float32 [8192], P('tp')
The draws below stay inside these ranges and needn't reach their ends.
All inputs are finite; a program needn't handle non-finite values.
Results may differ from the reference program's by a relative error of at most 0.015.
Values may be sent and summed in bfloat16 or wider, within the bound.
A program may use at most 128 MiB of HBM per device.

```python
import math
import jax
import jax.numpy as jnp
from jax import lax

D = 8192
MODES = 16
KS = 7
SEQ = 1024


def block_scale(rng, shape, split, low, top_value):
    def one(dim, shards_of):
        draws = jax.random.uniform(jax.random.fold_in(jax.random.fold_in(rng, 6), dim), (shards_of,), jnp.float32, low / len(split), top_value / len(split))
        return jnp.repeat(jnp.exp(draws), shape[dim] // shards_of).reshape((-1,) + (1,) * (len(shape) - dim - 1))

    loudness = one(*split[0])
    for cut in split[1:]:
        loudness = loudness * one(*cut)
    return loudness


def gaussian(rng, extent, width, limit, pieces=(), kind=jnp.bfloat16):
    level = block_scale(rng, extent, pieces, -0.22, 0.18) if pieces else 1.0
    values = jax.random.normal(rng, extent, jnp.float32) * width * level
    return jnp.minimum(jnp.maximum(values, -limit), limit).astype(kind)


def setup_inputs(seed: int = 0) -> dict:
    seeds = jax.random.split(jax.random.key(seed), 9)
    queries = gaussian(seeds[0], (D, SEQ), 1.0, 6.0, ((0, 4), (1, 8)))
    key_signal = gaussian(seeds[1], (D, SEQ), 1.0, 6.0, ((0, 4), (1, 8)))
    value_signal = gaussian(seeds[2], (D, SEQ), 1.0, 6.0, ((0, 4), (1, 8)))
    cotangent = gaussian(seeds[3], (D, SEQ), 1.0, 6.0, ((0, 4), (1, 8)))
    short_weight = gaussian(seeds[4], (3, KS, D), KS ** -0.5, 2.0, ((2, 4),), jnp.float32)
    residues = gaussian(seeds[5], (D, MODES), 0.25, 1.5, ((0, 4),), jnp.float32)
    decay_rates = jnp.clip(jnp.exp(math.log(0.03) - 5.7037825 * jax.random.uniform(seeds[6], (D, MODES), jnp.float32) ** block_scale(seeds[6], (D, MODES), ((0, 4),), -0.2, 0.2)), 0.0001, 0.03)
    skip_gain = jnp.clip(0.5 + 1.0 * jax.random.uniform(seeds[7], (D,), jnp.float32) ** block_scale(seeds[7], (D,), ((0, 4),), -0.2, 0.2), 0.5, 1.5)
    return dict(queries=queries, key_signal=key_signal, value_signal=value_signal, cotangent=cotangent, short_weight=short_weight, residues=residues, decay_rates=decay_rates, skip_gain=skip_gain)


def causal_taps(signal, weight):
    margin = weight.shape[0] - 1
    length = signal.shape[1]
    padded = jnp.pad(signal, ((0, 0), (margin, 0)))
    total = jnp.zeros(signal.shape, jnp.float32)
    for tap_index in range(weight.shape[0]):
        total = total + weight[tap_index][:, None] * padded[:, margin - tap_index:margin - tap_index + length]
    return total

def anti_taps(signal, weight):
    margin = weight.shape[0] - 1
    length = signal.shape[1]
    padded = jnp.pad(signal, ((0, 0), (0, margin)))
    total = jnp.zeros(signal.shape, jnp.float32)
    for tap_index in range(weight.shape[0]):
        total = total + weight[tap_index][:, None] * padded[:, tap_index:tap_index + length]
    return total

def tap_grads(grads, signal, taps):
    margin = taps - 1
    length = signal.shape[1]
    padded = jnp.pad(signal, ((0, 0), (margin, 0)))
    rows_out = []
    for tap_index in range(taps):
        rows_out.append(lax.optimization_barrier(jnp.sum(grads * padded[:, margin - tap_index:margin - tap_index + length], axis=1)))
    return jnp.stack(rows_out, 0)

def block_terms(operands):
    queries, key_signal, value_signal, cotangent, weights, residues, decay_rates, skip_gain = operands
    weights = jnp.transpose(weights, (1, 2, 0))
    q_in = queries.astype(jnp.float32)
    k_in = key_signal.astype(jnp.float32)
    v_in = value_signal.astype(jnp.float32)
    q_short = causal_taps(q_in, weights[0]).astype(jnp.bfloat16)
    k_short = causal_taps(k_in, weights[1]).astype(jnp.bfloat16)
    v_short = causal_taps(v_in, weights[2]).astype(jnp.bfloat16)
    gated = (k_short.astype(jnp.float32) * v_short.astype(jnp.float32)).astype(jnp.bfloat16)
    lags = jnp.arange(SEQ).astype(jnp.float32)
    powers = jnp.exp(-decay_rates[:, :, None] * lags)
    gain = residues * jnp.sqrt(2.0 * decay_rates)
    filt = jnp.einsum('bm,bmt->bt', gain, powers)
    spec_z = jnp.fft.rfft(gated.astype(jnp.float32), n=2 * SEQ, axis=1)
    spec_h = jnp.fft.rfft(filt, n=2 * SEQ, axis=1)
    conv = jnp.fft.irfft(spec_z * spec_h, n=2 * SEQ, axis=1)[:, :SEQ].astype(jnp.bfloat16)
    mix = conv.astype(jnp.float32) + skip_gain[:, None] * gated.astype(jnp.float32)
    mixed = (q_short.astype(jnp.float32) * mix).astype(jnp.bfloat16)
    cot = cotangent.astype(jnp.float32)
    grad_mix = (cot * q_short.astype(jnp.float32)).astype(jnp.bfloat16)
    grad_qshort = (cot * mix).astype(jnp.bfloat16)
    spec_g = jnp.fft.rfft(grad_mix.astype(jnp.float32), n=2 * SEQ, axis=1)
    grad_conv = jnp.fft.irfft(spec_g * jnp.conj(spec_h), n=2 * SEQ, axis=1)[:, :SEQ].astype(jnp.bfloat16)
    grad_gated = grad_conv.astype(jnp.float32) + skip_gain[:, None] * grad_mix.astype(jnp.float32)
    grad_kshort = (grad_gated * v_short.astype(jnp.float32)).astype(jnp.bfloat16)
    grad_vshort = (grad_gated * k_short.astype(jnp.float32)).astype(jnp.bfloat16)
    grad_queries = anti_taps(grad_qshort.astype(jnp.float32), weights[0]).astype(jnp.bfloat16)
    grad_keys = anti_taps(grad_kshort.astype(jnp.float32), weights[1]).astype(jnp.bfloat16)
    grad_values = anti_taps(grad_vshort.astype(jnp.float32), weights[2]).astype(jnp.bfloat16)
    scale = SEQ ** (-0.5)
    grad_short = jnp.stack([tap_grads(grad_qshort.astype(jnp.float32), q_in, KS), tap_grads(grad_kshort.astype(jnp.float32), k_in, KS), tap_grads(grad_vshort.astype(jnp.float32), v_in, KS)], 0) * scale
    grad_skip = lax.optimization_barrier(jnp.sum(grad_mix.astype(jnp.float32) * gated.astype(jnp.float32), axis=1)) * scale
    lag_sums = jnp.fft.irfft(spec_g * jnp.conj(spec_z), n=2 * SEQ, axis=1)[:, :SEQ]
    grad_residues = jnp.sqrt(2.0 * decay_rates) * jnp.einsum('bt,bmt->bm', lag_sums, powers) * scale
    return (mixed, grad_queries, grad_keys, grad_values, grad_short, grad_residues, grad_skip)

def reference(queries, key_signal, value_signal, cotangent, short_weight, residues, decay_rates, skip_gain):
    block = min(D, 128)
    count = D // block
    weights = jnp.transpose(short_weight, (2, 0, 1)).reshape(count, block, 3, KS)
    results = lax.map(block_terms, (queries.reshape(count, block, SEQ), key_signal.reshape(count, block, SEQ), value_signal.reshape(count, block, SEQ), cotangent.reshape(count, block, SEQ), weights, residues.reshape(count, block, MODES), decay_rates.reshape(count, block, MODES), skip_gain.reshape(count, block)))
    mixed, grad_queries, grad_keys, grad_values, grad_short, grad_residues, grad_skip = results
    grad_short = jnp.transpose(grad_short, (1, 2, 0, 3)).reshape(3, KS, D)
    return (mixed.reshape(D, SEQ), grad_queries.reshape(D, SEQ), grad_keys.reshape(D, SEQ), grad_values.reshape(D, SEQ), grad_short, grad_residues.reshape(D, MODES), grad_skip.reshape(D))
```

```python
import functools
import math

import jax
import jax.numpy as jnp
import ml_dtypes
import numpy as np
from jax import lax
from jax.experimental import pallas as pl
from jax.experimental.pallas import tpu as pltpu
from jax.sharding import PartitionSpec as P

F32 = jnp.float32
BF16 = jnp.bfloat16
NODES = 8
LANES = 128
BLOCK = 256
PAD = 8
MESH = pl.DeviceIdType.MESH


def two(table):
    high = table.astype(ml_dtypes.bfloat16)
    low = (table - high.astype(np.float64)).astype(ml_dtypes.bfloat16)
    return high, low


@functools.lru_cache(None)
def tables(rows, taps):
    top = rows - 1
    nodes = top / 2 - top / 2 * np.cos((2 * np.arange(NODES) + 1) * math.pi / (2 * NODES))
    spots = np.arange(rows, dtype=np.float64)
    basis = np.ones((NODES, rows))
    for k in range(NODES):
        for other in range(NODES):
            if other != k:
                basis[k] *= (spots - nodes[other]) / (nodes[k] - nodes[other])
    back = basis[:, ::-1]
    omega = 2 * math.pi * (np.arange(rows) + 0.5) / (2 * rows)
    angle = spots[:, None] * omega[None, :]
    dft = np.concatenate([np.cos(angle), -np.sin(angle)], 1)
    inv = dft / rows

    def three(table):
        high, low = two(table)
        return np.concatenate([high, high, low], 1)

    out = {}
    out["spec"] = three(dft.T @ basis.T)
    out["dft"] = two(dft.T)[0]
    out["inv"] = two(inv)[0]
    out["mom"] = np.concatenate(two(basis), 0)
    out["mom_back"] = np.concatenate(two(back), 0)
    out["lag"] = np.concatenate(two(basis @ inv), 0)
    out["far"] = three(basis.T)
    out["far_back"] = three(back.T)
    count = 3 * taps + 1
    pick = np.zeros((24, count * 8))
    for i in range(3):
        for j in range(taps):
            at = i * taps + j
            pick[i * 8 + j, at * 8 : at * 8 + 8] = 1
    pick[7, (count - 1) * 8 :] = 1
    out["pick"] = two(pick)[0]
    return [float(x) for x in nodes], out


def mm(a, b):
    return lax.dot_general(a, b, (((1,), (0,)), ((), ())), preferred_element_type=F32)


def mm_nt(a, b):
    return lax.dot_general(a, b, (((1,), (1,)), ((), ())), preferred_element_type=F32)


def stack3(x):
    high = x.astype(BF16).astype(F32)
    return jnp.concatenate([high, x - high, high], 0).astype(BF16)


def halves(x):
    return x[:NODES] + x[NODES:]


def pair(x):
    return jnp.concatenate([x[:, :LANES], x[:, LANES:]], 0)


def rows8(x):
    total = x[:8]
    for at in range(8, x.shape[0], 8):
        total = total + x[at : at + 8]
    return total


def main_kernel(nodes, taps, inside, scale,
                q_hbm, k_hbm, v_hbm, c_hbm, dec_ref, res_ref, w_ref, skip_ref,
                spec_ref, dft_ref, inv_ref, mom_ref, back_ref, lag_ref, far_ref, farb_ref, pick_ref,
                mixed_hbm, oq_hbm, ok_hbm, ov_hbm, short_ref, gres_ref, gskip_ref,
                xin, xs, cot, sh, gated, gmix, e_ref, h_ref, near, grad, resp, rmom, skp, gs, acc, obuf,
                tails, got_tails, heads, got_heads, moms, got_moms, parted, got_parts, mine, full,
                in_sem, out_sem, tail_sem, head_sem, mom_send, mom_recv, rs_send, rs_recv, ag_send, ag_recv):
    n = lax.axis_size("ctx")
    me = lax.axis_index("ctx")
    channels, rows = q_hbm.shape
    modes = dec_ref.shape[0]
    blocks = channels // BLOCK
    tiles = BLOCK // LANES
    where = [lax.rem(me + d, n) for d in range(n)]
    chunk_rows = 64
    chunks = range(0, rows, chunk_rows)

    loads = [pltpu.make_async_copy(ref, xin.at[i], in_sem.at[i]) for i, ref in enumerate((q_hbm, k_hbm, v_hbm, c_hbm))]
    for copy in loads:
        copy.start()
    barrier = pltpu.get_barrier_semaphore()
    for d in range(1, n):
        pl.semaphore_signal(barrier, inc=1, device_id={"ctx": where[d]}, device_id_type=MESH)

    def remote(src, dst, send_sem, recv_sem, d):
        return pltpu.make_async_remote_copy(
            src_ref=src, dst_ref=dst, send_sem=send_sem, recv_sem=recv_sem,
            device_id={"ctx": where[d]}, device_id_type=MESH)

    def each(body):
        lax.fori_loop(0, blocks, lambda b, c: (body(b), c)[1], 0)

    def cols(b):
        return pl.ds(pl.multiple_of(b * BLOCK, BLOCK), BLOCK)

    def lanes(b, h):
        return pl.ds(pl.multiple_of(b * BLOCK + h * LANES, LANES), LANES)

    eye = (lax.broadcasted_iota(jnp.int32, (rows, rows), 0) == lax.broadcasted_iota(jnp.int32, (rows, rows), 1)).astype(BF16)

    for copy in loads[:3]:
        copy.wait()

    def turn(b):
        for i in range(3):
            x = mm_nt(eye, xin[i, cols(b), :])
            for h in range(tiles):
                xs[i, b * tiles + h, PAD:, :] = x[:, h * LANES : (h + 1) * LANES]
            tails[i, b] = pair(x[rows - 8 :, :]).astype(BF16)

    each(turn)
    pl.semaphore_wait(barrier, n - 1)
    tail = remote(tails, got_tails, tail_sem.at[0], tail_sem.at[1], 1)
    tail.start()
    loads[3].wait()

    def prepare(b):
        at = cols(b)
        x = mm_nt(eye, xin[3, at, :])
        for h in range(tiles):
            cot[b * tiles + h] = x[:, h * LANES : (h + 1) * LANES]
        dec = dec_ref[:, at]
        gain = res_ref[:, at] * jnp.sqrt(2.0 * dec)
        row = lax.broadcasted_iota(jnp.int32, (NODES, BLOCK), 0)
        f = jnp.zeros((NODES, BLOCK), F32)
        for k in range(NODES):
            e = jnp.exp(dec * (-nodes[k]))
            e_ref[k, :, at] = e
            f = jnp.where(row == k, jnp.sum(gain * e, axis=0, keepdims=True), f)
        h_ref[b] = mm(spec_ref[...], stack3(f))

    each(prepare)
    tail.wait()

    def first(b):
        for i in range(3):
            halo = jnp.where(me > 0, got_tails[i, b].astype(F32), 0.0)
            for h in range(tiles):
                xs[i, b * tiles + h, :PAD, :] = halo[h * 8 : h * 8 + 8]
        for h in range(tiles):
            t = b * tiles + h
            skip_sum = jnp.zeros((8, LANES), F32)
            for r in chunks:
                short = []
                for i in range(3):
                    total = None
                    for j in range(taps):
                        term = w_ref[i, j : j + 1, lanes(b, h)] * xs[i, t, PAD + r - j : PAD + r - j + chunk_rows, :]
                        total = term if total is None else total + term
                    sh[i, t, r : r + chunk_rows, :] = total
                    short.append(total)
                x = short[1] * short[2]
                g = cot[t, r : r + chunk_rows, :] * short[0]
                gated[b, r : r + chunk_rows, h * LANES : (h + 1) * LANES] = x.astype(BF16)
                gmix[b, r : r + chunk_rows, h * LANES : (h + 1) * LANES] = g.astype(BF16)
                skip_sum = skip_sum + rows8(x * g)
            skp[t] = skip_sum
        moms[0, b] = pair(halves(mm(back_ref[...], gated[b]))).astype(BF16)
        r_mom = halves(mm(mom_ref[...], gmix[b]))
        rmom[b] = r_mom
        moms[1, b] = pair(r_mom).astype(BF16)

    each(first)
    states = []
    for d in range(1, n):
        kind = jnp.where(where[d] > me, 0, 1)
        copy = remote(moms.at[kind], got_moms.at[d], mom_send.at[d], mom_recv.at[d], d)
        copy.start()
        states.append(copy)

    def middle(b):
        z = mm(dft_ref[...], gated[b])
        g = mm(dft_ref[...], gmix[b])
        h = h_ref[b]
        zr, zi = z[:rows], z[rows:]
        gr, gi = g[:rows], g[rows:]
        hr, hi = h[:rows], h[rows:]
        fwd = jnp.concatenate([zr * hr - zi * hi, zr * hi + zi * hr], 0).astype(BF16)
        bwd = jnp.concatenate([gr * hr + gi * hi, gi * hr - gr * hi], 0).astype(BF16)
        lag = jnp.concatenate([gr * zr + gi * zi, gi * zr - gr * zi], 0).astype(BF16)
        near[b] = mm(inv_ref[...], fwd)
        grad[b] = mm(inv_ref[...], bwd)
        moments = halves(mm(lag_ref[...], lag))
        total = jnp.zeros((modes, BLOCK), F32)
        for k in range(NODES):
            total = total + e_ref[k, :, cols(b)] * moments[k : k + 1, :]
        resp[:, cols(b)] = total

    each(middle)
    for copy in states:
        copy.wait()

    def last(b):
        at = cols(b)
        dec = dec_ref[:, at]
        root = jnp.sqrt(2.0 * dec)
        one = jnp.exp(-dec)
        chunk = jnp.exp(dec * (-float(rows)))
        es = [e_ref[k, :, at] for k in range(NODES)]

        def spread(x):
            total = es[0] * x[0:1, :]
            for k in range(1, NODES):
                total = total + es[k] * x[k : k + 1, :]
            return total

        def carry(d, s):
            raw = got_moms[d, b].astype(F32)
            new = spread(jnp.concatenate([raw[:NODES], raw[NODES:]], 1))
            return s * chunk + new

        s = jnp.zeros((modes, BLOCK), F32)
        r = jnp.zeros((modes, BLOCK), F32)
        s = lax.fori_loop(0, me, lambda i, s: carry(me - i, s), s)
        r = lax.fori_loop(me + 1, n, lambda i, r: carry(i, r), r)
        own = root * (resp[:, at] + one * s * spread(rmom[b]))
        gain = res_ref[:, at] * root * one
        row = lax.broadcasted_iota(jnp.int32, (NODES, BLOCK), 0)
        fs = jnp.zeros((NODES, BLOCK), F32)
        fr = jnp.zeros((NODES, BLOCK), F32)
        gain_s, gain_r = gain * s, gain * r
        for k in range(NODES):
            fs = jnp.where(row == k, jnp.sum(gain_s * es[k], axis=0, keepdims=True), fs)
            fr = jnp.where(row == k, jnp.sum(gain_r * es[k], axis=0, keepdims=True), fr)
        near[b] = near[b] + mm(far_ref[...], stack3(fs))
        grad[b] = grad[b] + mm(farb_ref[...], stack3(fr))
        mixed = []
        for h in range(tiles):
            t = b * tiles + h
            hl = slice(h * LANES, (h + 1) * LANES)
            skip = skip_ref[:, lanes(b, h)]
            sums = [jnp.zeros((8, LANES), F32)] * (3 * taps)
            out = []
            for r0 in chunks:
                rr = slice(r0, r0 + chunk_rows)
                qs, ks, vs = (sh[i, t, rr, :] for i in range(3))
                c = cot[t, rr, :]
                mix = near[b, rr, hl] + skip * (ks * vs)
                back = grad[b, rr, hl] + skip * (c * qs)
                out.append(qs * mix)
                grads = (c * mix, back * vs, back * ks)
                for i in range(3):
                    gs[i, t, rr, :] = grads[i]
                    for j in range(taps):
                        shifted = xs[i, t, PAD + r0 - j : PAD + r0 - j + chunk_rows, :]
                        sums[i * taps + j] = sums[i * taps + j] + rows8(grads[i] * shifted)
            obuf[0, lanes(b, h), :] = jnp.concatenate(out, 0).T.astype(BF16)
            for a in range(3 * taps):
                acc[a * 8 : a * 8 + 8, hl] = sums[a]
            acc[3 * taps * 8 :, hl] = skp[t]
        for i in range(3):
            heads[i, b] = jnp.concatenate([gs[i, b * tiles + h, :8, :] for h in range(tiles)], 0).astype(BF16)
        total = jnp.concatenate([own, mm(pick_ref[...], acc[...].astype(BF16))], 0)
        if inside:
            parted[b] = pair(total).astype(BF16)
        else:
            gres_ref[:, at] = total[:modes]
            for i in range(3):
                short_ref[i, :, at] = total[modes + 8 * i : modes + 8 * i + taps]
            gskip_ref[:, at] = total[modes + 7 : modes + 8]
        pltpu.make_async_copy(obuf.at[0, at, :], mixed_hbm.at[at, :], out_sem.at[0, b]).start()

    each(last)
    head = remote(heads, got_heads, head_sem.at[0], head_sem.at[1], n - 1)
    head.start()
    pieces = []
    if inside:
        for d in range(1, n):
            copy = remote(parted.at[where[d]], got_parts.at[d], rs_send.at[d], rs_recv.at[d], d)
            copy.start()
            pieces.append(copy)
    head.wait()

    def final(b):
        at = cols(b)
        for i in range(3):
            halo = jnp.where(me < n - 1, got_heads[i, b].astype(F32), 0.0)
            for h in range(tiles):
                gs[i, b * tiles + h, rows:, :] = halo[h * 8 : h * 8 + 8]
        for h in range(tiles):
            t = b * tiles + h
            for i in range(3):
                out = []
                for r in chunks:
                    total = None
                    for j in range(taps):
                        term = w_ref[i, j : j + 1, lanes(b, h)] * gs[i, t, r + j : r + j + chunk_rows, :]
                        total = term if total is None else total + term
                    out.append(total)
                obuf[i + 1, lanes(b, h), :] = jnp.concatenate(out, 0).T.astype(BF16)
        for i, ref in enumerate((oq_hbm, ok_hbm, ov_hbm)):
            pltpu.make_async_copy(obuf.at[i + 1, at, :], ref.at[at, :], out_sem.at[i + 1, b]).start()

    half = blocks // 2
    lax.fori_loop(0, half, lambda b, c: (final(b), c)[1], 0)
    if inside:
        total = parted[me].astype(F32)
        for d in range(1, n):
            pieces[d - 1].wait()
            total = total + got_parts[d].astype(F32)
        mine[...] = (total * scale).astype(BF16)
        pieces = []
        for d in range(1, n):
            copy = remote(mine, full.at[d], ag_send.at[d], ag_recv.at[d], d)
            copy.start()
            pieces.append(copy)
        full[0] = mine[...]
    lax.fori_loop(half, blocks, lambda b, c: (final(b), c)[1], 0)
    if inside:
        for copy in pieces:
            copy.wait()
        height = modes + 24
        for p in range(n):
            value = full[lax.rem(me - p + n, n)].astype(F32)
            for h in range(tiles):
                x = value[h * height : (h + 1) * height]
                hl = slice(p * BLOCK + h * LANES, p * BLOCK + (h + 1) * LANES)
                gres_ref[:, hl] = x[:modes]
                for i in range(3):
                    short_ref[i, :, hl] = x[modes + 8 * i : modes + 8 * i + taps]
                gskip_ref[:, hl] = x[modes + 7 : modes + 8]

    def finish(b):
        for i, ref in enumerate((mixed_hbm, oq_hbm, ok_hbm, ov_hbm)):
            pltpu.make_async_copy(obuf.at[i, cols(b), :], ref.at[cols(b), :], out_sem.at[i, b]).wait()

    each(finish)


def per_device(queries, key_signal, value_signal, cotangent, short_weight, residues, decay_rates, skip_gain):
    channels, rows = queries.shape
    taps = short_weight.shape[1]
    modes = residues.shape[1]
    n = lax.axis_size("ctx")
    nodes, tab = tables(rows, taps)
    blocks, count = channels // BLOCK, channels // LANES
    inside = channels // n == BLOCK
    scale = 1.0 / math.sqrt(rows * n)
    height = 2 * (modes + 24)
    dma = pltpu.SemaphoreType.DMA

    def shape(*dims, kind=F32):
        return jax.ShapeDtypeStruct(dims, kind)

    vmem = pl.BlockSpec(memory_space=pltpu.VMEM)
    hbm = pl.BlockSpec(memory_space=pl.ANY)
    names = ("spec", "dft", "inv", "mom", "mom_back", "lag", "far", "far_back", "pick")
    args = [jnp.asarray(tab[name]) for name in names]
    owners = n if inside else 1
    mixed, gq, gk, gv, short, gres, gskip = pl.pallas_call(
        functools.partial(main_kernel, nodes, taps, inside, scale),
        in_specs=[hbm] * 4 + [vmem] * (4 + len(args)),
        out_specs=[hbm] * 4 + [vmem] * 3,
        out_shape=[shape(channels, rows, kind=BF16)] * 4 + [shape(3, taps, channels), shape(modes, channels), shape(1, channels)],
        scratch_shapes=[
            pltpu.VMEM((4, channels, rows), BF16),
            pltpu.VMEM((3, count, rows + PAD, LANES), F32),
            pltpu.VMEM((count, rows, LANES), F32),
            pltpu.VMEM((3, count, rows, LANES), F32),
            pltpu.VMEM((blocks, rows, BLOCK), BF16),
            pltpu.VMEM((blocks, rows, BLOCK), BF16),
            pltpu.VMEM((NODES, modes, channels), F32),
            pltpu.VMEM((blocks, 2 * rows, BLOCK), F32),
            pltpu.VMEM((blocks, rows, BLOCK), F32),
            pltpu.VMEM((blocks, rows, BLOCK), F32),
            pltpu.VMEM((modes, channels), F32),
            pltpu.VMEM((blocks, NODES, BLOCK), F32),
            pltpu.VMEM((count, 8, LANES), F32),
            pltpu.VMEM((3, count, rows + PAD, LANES), F32),
            pltpu.VMEM((8 * (3 * taps + 1), BLOCK), F32),
            pltpu.VMEM((4, channels, rows), BF16),
            pltpu.VMEM((3, blocks, 16, LANES), BF16),
            pltpu.VMEM((3, blocks, 16, LANES), BF16),
            pltpu.VMEM((3, blocks, 16, LANES), BF16),
            pltpu.VMEM((3, blocks, 16, LANES), BF16),
            pltpu.VMEM((2, blocks, 16, LANES), BF16),
            pltpu.VMEM((n, blocks, 16, LANES), BF16),
            pltpu.VMEM((owners, height, LANES), BF16),
            pltpu.VMEM((owners, height, LANES), BF16),
            pltpu.VMEM((height, LANES), BF16),
            pltpu.VMEM((owners, height, LANES), BF16),
            dma((4,)), dma((4, blocks)), dma((2,)), dma((2,)),
            dma((n,)), dma((n,)), dma((owners,)), dma((owners,)), dma((owners,)), dma((owners,)),
        ],
        compiler_params=pltpu.CompilerParams(collective_id=0, has_side_effects=True, vmem_limit_bytes=60 * 1024 * 1024),
        cost_estimate=pl.CostEstimate(flops=4 * 10**9, bytes_accessed=5 * 10**6, transcendentals=3 * 10**5),
        name="hyena",
    )(queries, key_signal, value_signal, cotangent, decay_rates.T, residues.T, short_weight, skip_gain[None, :], *args)
    if not inside:
        short, gres, gskip = (lax.psum(x, "ctx") * scale for x in (short, gres, gskip))
    return mixed, gq, gk, gv, short, gres.T, gskip[0]


def solution(mesh):
    signal = P("tp", "ctx")
    in_specs = (signal,) * 4 + (P(None, None, "tp"), P("tp", None), P("tp", None), P("tp"))
    out_specs = (signal,) * 4 + (P(None, None, "tp"), P("tp", None), P("tp"))
    return jax.shard_map(
        per_device, mesh=mesh, in_specs=in_specs, out_specs=out_specs, check_vma=False
    )
```

```python
import functools
import math

import jax
import jax.numpy as jnp
import ml_dtypes
import numpy as np
from jax import lax
from jax.experimental import pallas as pl
from jax.experimental.pallas import tpu as pltpu
from jax.sharding import PartitionSpec as P

F32 = jnp.float32
BF16 = jnp.bfloat16
NODES = 8
LANES = 128
BLOCK = 256
STRIP = 64
PAD = 8
MESH = pl.DeviceIdType.MESH


def two(table):
    high = table.astype(ml_dtypes.bfloat16)
    low = (table - high.astype(np.float64)).astype(ml_dtypes.bfloat16)
    return high, low


@functools.lru_cache(None)
def tables(rows, taps):
    top = rows - 1
    nodes = top / 2 - top / 2 * np.cos((2 * np.arange(NODES) + 1) * math.pi / (2 * NODES))
    spots = np.arange(rows, dtype=np.float64)
    basis = np.ones((NODES, rows))
    for k in range(NODES):
        for other in range(NODES):
            if other != k:
                basis[k] *= (spots - nodes[other]) / (nodes[k] - nodes[other])
    back = basis[:, ::-1]
    omega = 2 * math.pi * (np.arange(rows) + 0.5) / (2 * rows)
    angle = spots[:, None] * omega[None, :]
    dft = np.concatenate([np.cos(angle), -np.sin(angle)], 1)
    inv = dft / rows

    def three(table):
        high, low = two(table)
        return np.concatenate([high, high, low], 1)

    out = {}
    out["spec"] = three(dft.T @ basis.T)
    out["dft"] = two(dft.T)[0]
    out["inv"] = two(inv)[0]
    out["mom"] = np.concatenate(two(basis), 0)
    out["mom_back"] = np.concatenate(two(back), 0)
    out["lag"] = np.concatenate(two(basis @ inv), 0)
    out["far"] = three(basis.T)
    out["far_back"] = three(back.T)
    count = 3 * taps + 1
    pick = np.zeros((24, count * 8))
    for i in range(3):
        for j in range(taps):
            at = i * taps + j
            pick[i * 8 + j, at * 8 : at * 8 + 8] = 1
    pick[7, (count - 1) * 8 :] = 1
    out["pick"] = two(pick)[0]
    return [float(x) for x in nodes], out


def mm(a, b):
    return lax.dot_general(a, b, (((1,), (0,)), ((), ())), preferred_element_type=F32)


def mm_nt(a, b):
    return lax.dot_general(a, b, (((1,), (1,)), ((), ())), preferred_element_type=F32)


def stack3(x):
    high = x.astype(BF16).astype(F32)
    return jnp.concatenate([high, x - high, high], 0).astype(BF16)


def halves(x):
    return x[:NODES] + x[NODES:]


def pair(x):
    return jnp.concatenate([x[:, :LANES], x[:, LANES:]], 0)


def rows8(x):
    total = x[:8]
    for at in range(8, x.shape[0], 8):
        total = total + x[at : at + 8]
    return total


def main_kernel(nodes, taps, inside, scale,
                q_hbm, k_hbm, v_hbm, c_hbm, dec_ref, res_ref, w_ref, skip_ref,
                spec_ref, dft_ref, inv_ref, mom_ref, back_ref, lag_ref, far_ref, farb_ref, pick_ref,
                mixed_ref, oq_ref, ok_ref, ov_ref, short_ref, gres_ref, gskip_ref,
                xin, xs, cot, sh, gated, gmix, e_ref, h_ref, near, grad, resp, rmom, skp, gs, acc, far,
                tails, got_tails, heads, got_heads, moms, got_moms, parted, got_parts, mine, full,
                in_sem, tail_sem, head_sem, mom_send, mom_recv, rs_send, rs_recv, ag_send, ag_recv):
    n = lax.axis_size("ctx")
    me = lax.axis_index("ctx")
    channels, rows = q_hbm.shape
    modes = dec_ref.shape[0]
    blocks = channels // BLOCK
    tiles = BLOCK // LANES
    where = [lax.rem(me + d, n) for d in range(n)]

    loads = [pltpu.make_async_copy(ref, xin.at[i], in_sem.at[i]) for i, ref in enumerate((q_hbm, k_hbm, v_hbm, c_hbm))]
    for copy in loads:
        copy.start()
    barrier = pltpu.get_barrier_semaphore()
    for d in range(1, n):
        pl.semaphore_signal(barrier, inc=1, device_id={"ctx": where[d]}, device_id_type=MESH)

    def remote(src, dst, send_sem, recv_sem, d):
        return pltpu.make_async_remote_copy(
            src_ref=src, dst_ref=dst, send_sem=send_sem, recv_sem=recv_sem,
            device_id={"ctx": where[d]}, device_id_type=MESH)

    def each(body):
        lax.fori_loop(0, blocks, lambda b, c: (body(b), c)[1], 0, unroll=True)

    def cols(b):
        return pl.ds(pl.multiple_of(b * BLOCK, BLOCK), BLOCK)

    def lanes(b, h):
        return pl.ds(pl.multiple_of(b * BLOCK + h * LANES, LANES), LANES)

    eye = (lax.broadcasted_iota(jnp.int32, (rows, rows), 0) == lax.broadcasted_iota(jnp.int32, (rows, rows), 1)).astype(BF16)

    for copy in loads[:3]:
        copy.wait()

    def turn(b):
        for i in range(3):
            x = mm_nt(eye, xin[i, cols(b), :])
            for h in range(tiles):
                xs[i, b * tiles + h, PAD:, :] = x[:, h * LANES : (h + 1) * LANES]
            tails[i, b] = pair(x[rows - 8 :, :]).astype(BF16)

    each(turn)
    pl.semaphore_wait(barrier, n - 1)
    tail = remote(tails, got_tails, tail_sem.at[0], tail_sem.at[1], 1)
    tail.start()
    loads[3].wait()

    def prepare(b):
        at = cols(b)
        x = mm_nt(eye, xin[3, at, :])
        for h in range(tiles):
            cot[b * tiles + h] = x[:, h * LANES : (h + 1) * LANES]
        dec = dec_ref[:, at]
        gain = res_ref[:, at] * jnp.sqrt(2.0 * dec)
        row = lax.broadcasted_iota(jnp.int32, (NODES, BLOCK), 0)
        f = jnp.zeros((NODES, BLOCK), F32)
        for k in range(NODES):
            e = jnp.exp(dec * (-nodes[k]))
            e_ref[k, :, at] = e
            f = jnp.where(row == k, jnp.sum(gain * e, axis=0, keepdims=True), f)
        h_ref[b] = mm(spec_ref[...], stack3(f))

    each(prepare)
    tail.wait()

    def first(b):
        for i in range(3):
            halo = jnp.where(me > 0, got_tails[i, b].astype(F32), 0.0)
            for h in range(tiles):
                xs[i, b * tiles + h, :PAD, :] = halo[h * 8 : h * 8 + 8]
        for h in range(tiles):
            t = b * tiles + h
            skip_sum = jnp.zeros((8, LANES), F32)
            for r in range(0, rows, STRIP):
                short = []
                for i in range(3):
                    total = None
                    for j in range(taps):
                        term = w_ref[i, j : j + 1, lanes(b, h)] * xs[i, t, PAD + r - j : PAD + r - j + STRIP, :]
                        total = term if total is None else total + term
                    sh[i, t, r : r + STRIP, :] = total
                    short.append(total)
                x = short[1] * short[2]
                g = cot[t, r : r + STRIP, :] * short[0]
                gated[b, r : r + STRIP, h * LANES : (h + 1) * LANES] = x.astype(BF16)
                gmix[b, r : r + STRIP, h * LANES : (h + 1) * LANES] = g.astype(BF16)
                skip_sum = skip_sum + rows8(x * g)
            skp[t] = skip_sum
        moms[0, b] = pair(halves(mm(back_ref[...], gated[b]))).astype(BF16)
        r_mom = halves(mm(mom_ref[...], gmix[b]))
        rmom[b] = r_mom
        moms[1, b] = pair(r_mom).astype(BF16)

    each(first)
    states = []
    for d in range(1, n):
        kind = jnp.where(where[d] > me, 0, 1)
        copy = remote(moms.at[kind], got_moms.at[d], mom_send.at[d], mom_recv.at[d], d)
        copy.start()
        states.append(copy)

    def middle(b):
        z = mm(dft_ref[...], gated[b])
        g = mm(dft_ref[...], gmix[b])
        h = h_ref[b]
        zr, zi = z[:rows], z[rows:]
        gr, gi = g[:rows], g[rows:]
        hr, hi = h[:rows], h[rows:]
        fwd = jnp.concatenate([zr * hr - zi * hi, zr * hi + zi * hr], 0).astype(BF16)
        bwd = jnp.concatenate([gr * hr + gi * hi, gi * hr - gr * hi], 0).astype(BF16)
        lag = jnp.concatenate([gr * zr + gi * zi, gi * zr - gr * zi], 0).astype(BF16)
        near[b] = mm(inv_ref[...], fwd)
        grad[b] = mm(inv_ref[...], bwd)
        moments = halves(mm(lag_ref[...], lag))
        total = jnp.zeros((modes, BLOCK), F32)
        for k in range(NODES):
            total = total + e_ref[k, :, cols(b)] * moments[k : k + 1, :]
        resp[:, cols(b)] = total

    each(middle)
    for copy in states:
        copy.wait()

    def arrive(b):
        at = cols(b)
        dec = dec_ref[:, at]
        root = jnp.sqrt(2.0 * dec)
        one = jnp.exp(-dec)
        chunk = jnp.exp(dec * (-float(rows)))
        es = [e_ref[k, :, at] for k in range(NODES)]

        def spread(x):
            total = es[0] * x[0:1, :]
            for k in range(1, NODES):
                total = total + es[k] * x[k : k + 1, :]
            return total

        def arrived(d):
            raw = got_moms[d, b].astype(F32)
            return spread(jnp.concatenate([raw[:NODES], raw[NODES:]], 1))

        s = r = jnp.zeros((modes, BLOCK), F32)
        if n <= 8:
            new = [arrived(d) for d in range(1, n)]
            for d in range(n - 1, 0, -1):
                s = jnp.where(me >= d, s * chunk + new[d - 1], s)
            for d in range(1, n):
                r = jnp.where(me < d, r * chunk + new[d - 1], r)
        else:
            s = lax.fori_loop(0, me, lambda i, s: s * chunk + arrived(me - i), s)
            r = lax.fori_loop(me + 1, n, lambda i, r: r * chunk + arrived(i), r)
        resp[:, at] = root * (resp[:, at] + one * s * spread(rmom[b]))
        gain = res_ref[:, at] * root * one
        row = lax.broadcasted_iota(jnp.int32, (NODES, BLOCK), 0)
        fs = jnp.zeros((NODES, BLOCK), F32)
        fr = jnp.zeros((NODES, BLOCK), F32)
        gain_s, gain_r = gain * s, gain * r
        for k in range(NODES):
            fs = jnp.where(row == k, jnp.sum(gain_s * es[k], axis=0, keepdims=True), fs)
            fr = jnp.where(row == k, jnp.sum(gain_r * es[k], axis=0, keepdims=True), fr)
        far[0, b] = stack3(fs)
        far[1, b] = stack3(fr)

    each(arrive)

    def last(b):
        at = cols(b)
        near[b] = near[b] + mm(far_ref[...], far[0, b])
        grad[b] = grad[b] + mm(farb_ref[...], far[1, b])
        for h in range(tiles):
            t = b * tiles + h
            hl = slice(h * LANES, (h + 1) * LANES)
            skip = skip_ref[:, lanes(b, h)]
            sums = [jnp.zeros((8, LANES), F32)] * (3 * taps)
            out = []
            for r0 in range(0, rows, STRIP):
                rr = slice(r0, r0 + STRIP)
                qs, ks, vs = (sh[i, t, rr, :] for i in range(3))
                c = cot[t, rr, :]
                mix = near[b, rr, hl] + skip * (ks * vs)
                back = grad[b, rr, hl] + skip * (c * qs)
                out.append(qs * mix)
                grads = (c * mix, back * vs, back * ks)
                for i in range(3):
                    gs[i, t, rr, :] = grads[i]
                    for j in range(taps):
                        shifted = xs[i, t, PAD + r0 - j : PAD + r0 - j + STRIP, :]
                        sums[i * taps + j] = sums[i * taps + j] + rows8(grads[i] * shifted)
            mixed_ref[lanes(b, h), :] = jnp.concatenate(out, 0).T.astype(BF16)
            for a in range(3 * taps):
                acc[a * 8 : a * 8 + 8, hl] = sums[a]
            acc[3 * taps * 8 :, hl] = skp[t]
        for i in range(3):
            heads[i, b] = jnp.concatenate([gs[i, b * tiles + h, :8, :] for h in range(tiles)], 0).astype(BF16)
        total = jnp.concatenate([resp[:, at], mm(pick_ref[...], acc[...].astype(BF16))], 0)
        if inside:
            parted[b] = pair(total).astype(BF16)
        else:
            gres_ref[:, at] = total[:modes]
            for i in range(3):
                short_ref[i, :, at] = total[modes + 8 * i : modes + 8 * i + taps]
            gskip_ref[:, at] = total[modes + 7 : modes + 8]

    each(last)
    head = remote(heads, got_heads, head_sem.at[0], head_sem.at[1], n - 1)
    head.start()
    pieces = []
    if inside:
        for d in range(1, n):
            copy = remote(parted.at[where[d]], got_parts.at[d], rs_send.at[d], rs_recv.at[d], d)
            copy.start()
            pieces.append(copy)
    head.wait()

    outs = (oq_ref, ok_ref, ov_ref)

    def final(b):
        at = cols(b)
        for i in range(3):
            halo = jnp.where(me < n - 1, got_heads[i, b].astype(F32), 0.0)
            for h in range(tiles):
                gs[i, b * tiles + h, rows:, :] = halo[h * 8 : h * 8 + 8]
        for h in range(tiles):
            t = b * tiles + h
            for i in range(3):
                out = []
                for r in range(0, rows, STRIP):
                    total = None
                    for j in range(taps):
                        term = w_ref[i, j : j + 1, lanes(b, h)] * gs[i, t, r + j : r + j + STRIP, :]
                        total = term if total is None else total + term
                    out.append(total)
                outs[i][lanes(b, h), :] = jnp.concatenate(out, 0).T.astype(BF16)

    half = blocks // 2
    lax.fori_loop(0, half, lambda b, c: (final(b), c)[1], 0, unroll=True)
    if inside:
        total = parted[me].astype(F32)
        for d in range(1, n):
            pieces[d - 1].wait()
            total = total + got_parts[d].astype(F32)
        mine[...] = (total * scale).astype(BF16)
        pieces = []
        for d in range(1, n):
            copy = remote(mine, full.at[d], ag_send.at[d], ag_recv.at[d], d)
            copy.start()
            pieces.append(copy)
        full[0] = mine[...]
    lax.fori_loop(half, blocks, lambda b, c: (final(b), c)[1], 0, unroll=True)
    if inside:
        for copy in pieces:
            copy.wait()
        height = modes + 24
        for p in range(n):
            value = full[lax.rem(me - p + n, n)].astype(F32)
            for h in range(tiles):
                x = value[h * height : (h + 1) * height]
                hl = slice(p * BLOCK + h * LANES, p * BLOCK + (h + 1) * LANES)
                gres_ref[:, hl] = x[:modes]
                for i in range(3):
                    short_ref[i, :, hl] = x[modes + 8 * i : modes + 8 * i + taps]
                gskip_ref[:, hl] = x[modes + 7 : modes + 8]


def output_kernel(*refs):
    count = (len(refs) - 1) // 2
    sems = refs[-1]
    copies = [pltpu.make_async_copy(refs[i], refs[count + i], sems.at[i]) for i in range(count)]
    for copy in copies:
        copy.start()
    for copy in copies:
        copy.wait()


def per_device(queries, key_signal, value_signal, cotangent, short_weight, residues, decay_rates, skip_gain):
    channels, rows = queries.shape
    taps = short_weight.shape[1]
    modes = residues.shape[1]
    n = lax.axis_size("ctx")
    nodes, tab = tables(rows, taps)
    blocks, count = channels // BLOCK, channels // LANES
    inside = channels // n == BLOCK
    scale = 1.0 / math.sqrt(rows * n)
    height = 2 * (modes + 24)
    dma = pltpu.SemaphoreType.DMA

    def shape(*dims, kind=F32):
        return jax.ShapeDtypeStruct(dims, kind)

    vmem = pl.BlockSpec(memory_space=pltpu.VMEM)
    hbm = pl.BlockSpec(memory_space=pl.ANY)
    names = ("spec", "dft", "inv", "mom", "mom_back", "lag", "far", "far_back", "pick")
    args = [jnp.asarray(tab[name]) for name in names]
    owners = n if inside else 1
    mixed, gq, gk, gv, short, gres, gskip = pl.pallas_call(
        functools.partial(main_kernel, nodes, taps, inside, scale),
        in_specs=[hbm] * 4 + [vmem] * (4 + len(args)),
        out_specs=[vmem] * 7,
        out_shape=[pltpu.VMEM((channels, rows), BF16)] * 4 + [pltpu.VMEM((3, taps, channels), F32), pltpu.VMEM((modes, channels), F32), pltpu.VMEM((1, channels), F32)],
        scratch_shapes=[
            pltpu.VMEM((4, channels, rows), BF16),
            pltpu.VMEM((3, count, rows + PAD, LANES), F32),
            pltpu.VMEM((count, rows, LANES), F32),
            pltpu.VMEM((3, count, rows, LANES), F32),
            pltpu.VMEM((blocks, rows, BLOCK), BF16),
            pltpu.VMEM((blocks, rows, BLOCK), BF16),
            pltpu.VMEM((NODES, modes, channels), F32),
            pltpu.VMEM((blocks, 2 * rows, BLOCK), F32),
            pltpu.VMEM((blocks, rows, BLOCK), F32),
            pltpu.VMEM((blocks, rows, BLOCK), F32),
            pltpu.VMEM((modes, channels), F32),
            pltpu.VMEM((blocks, NODES, BLOCK), F32),
            pltpu.VMEM((count, 8, LANES), F32),
            pltpu.VMEM((3, count, rows + PAD, LANES), F32),
            pltpu.VMEM((8 * (3 * taps + 1), BLOCK), F32),
            pltpu.VMEM((2, blocks, 3 * NODES, BLOCK), BF16),
            pltpu.VMEM((3, blocks, 16, LANES), BF16),
            pltpu.VMEM((3, blocks, 16, LANES), BF16),
            pltpu.VMEM((3, blocks, 16, LANES), BF16),
            pltpu.VMEM((3, blocks, 16, LANES), BF16),
            pltpu.VMEM((2, blocks, 16, LANES), BF16),
            pltpu.VMEM((n, blocks, 16, LANES), BF16),
            pltpu.VMEM((owners, height, LANES), BF16),
            pltpu.VMEM((owners, height, LANES), BF16),
            pltpu.VMEM((height, LANES), BF16),
            pltpu.VMEM((owners, height, LANES), BF16),
            dma((4,)), dma((2,)), dma((2,)),
            dma((n,)), dma((n,)), dma((owners,)), dma((owners,)), dma((owners,)), dma((owners,)),
        ],
        compiler_params=pltpu.CompilerParams(collective_id=0, has_side_effects=True, vmem_limit_bytes=60 * 1024 * 1024),
        cost_estimate=pl.CostEstimate(flops=4 * 10**9, bytes_accessed=5 * 10**6, transcendentals=3 * 10**5),
        name="hyena",
    )(queries, key_signal, value_signal, cotangent, decay_rates.T, residues.T, short_weight, skip_gain[None, :], *args)
    if not inside:
        short, gres, gskip = (lax.psum(x, "ctx") * scale for x in (short, gres, gskip))
    else:
        values = (mixed, gq, gk, gv, short, gres, gskip)
        mixed, gq, gk, gv, short, gres, gskip = pl.pallas_call(
            output_kernel,
            in_specs=[vmem] * 7,
            out_specs=[hbm] * 7,
            out_shape=[shape(*x.shape, kind=x.dtype) for x in values],
            scratch_shapes=[dma((7,))],
            name="output",
        )(*[pltpu.with_memory_space_constraint(x, pltpu.VMEM) for x in values])
    return mixed, gq, gk, gv, short, gres.T, gskip[0]


def solution(mesh):
    signal = P("tp", "ctx")
    in_specs = (signal,) * 4 + (P(None, None, "tp"), P("tp", None), P("tp", None), P("tp"))
    out_specs = (signal,) * 4 + (P(None, None, "tp"), P("tp", None), P("tp"))
    return jax.shard_map(
        per_device, mesh=mesh, in_specs=in_specs, out_specs=out_specs, check_vma=False
    )
```

```python
import functools
import math

import jax
import jax.numpy as jnp
import ml_dtypes
import numpy as np
from jax import lax
from jax.experimental import pallas as pl
from jax.experimental.pallas import tpu as pltpu
from jax.sharding import PartitionSpec as P

F32 = jnp.float32
BF16 = jnp.bfloat16
NODES = 8
LANES = 128
SMALLS = 13
MAX_DECAY = 0.03
BLOCK = 256
STRIP = 64
EDGE = 16
PAD = 8
MESH = pl.DeviceIdType.MESH


def two(table):
    high = table.astype(ml_dtypes.bfloat16)
    low = (table - high.astype(np.float64)).astype(ml_dtypes.bfloat16)
    return high, low


@functools.lru_cache(None)
def tables(rows, taps, modes):
    top = rows - 1
    points = -np.cos((2 * np.arange(NODES) + 1) * math.pi / (2 * NODES))
    order = np.arange(NODES)

    def cheb(y):
        return np.cos(order[:, None] * np.arccos(y)[None, :])

    nodes = top / 2 * (1 + points)
    turn = cheb(points) * (2 - (order == 0))[:, None] / NODES
    spots = np.arange(rows, dtype=np.float64)
    basis = cheb(spots / (top / 2) - 1)
    decays = np.linspace(0, MAX_DECAY, 401)
    shares = np.abs(turn @ np.exp(-nodes[:, None] * decays))
    reach = []
    for distance in range(1, 8):
        left = np.cumsum((shares * np.exp(-decays * rows * (distance - 1)))[::-1], 0)[::-1].max(1)
        reach.append(NODES if distance == 1 else int(next(j for j in range(NODES + 1) if j == NODES or left[j] < 1e-5)))
    back = basis[:, ::-1]
    omega = 2 * math.pi * (np.arange(rows) + 0.5) / (2 * rows)
    angle = spots[:, None] * omega[None, :]
    dft = np.concatenate([np.cos(angle), -np.sin(angle)], 1)
    inv = dft / rows

    def wide(table):
        return two(np.repeat(table, modes, 1))[0]

    out = {}
    out["spec"] = wide(dft.T @ basis.T)
    out["dft"] = two(dft.T)[0]
    out["inv"] = two(inv)[0]
    out["mom"] = np.concatenate(two(basis), 0)
    out["mom_back"] = np.concatenate(two(back), 0)
    out["lag"] = np.concatenate(two(basis @ inv), 0)
    out["far"] = wide(basis.T)
    out["far_back"] = wide(back.T)
    count = 3 * taps + 1
    pick = np.zeros((24, count * 8))
    for i in range(3):
        for j in range(taps):
            at = i * taps + j
            pick[i * 8 + j, at * 8 : at * 8 + 8] = 1
    pick[7, (count - 1) * 8 :] = 1
    out["pick"] = two(pick)[0]
    return (nodes.tolist(), turn.tolist(), reach), out


def mm(a, b):
    return lax.dot_general(a, b, (((1,), (0,)), ((), ())), preferred_element_type=F32)


def mm_nt(a, b):
    return lax.dot_general(a, b, (((1,), (1,)), ((), ())), preferred_element_type=F32)


def halves(x):
    return x[:NODES] + x[NODES:]


def pair(x):
    return jnp.concatenate([x[:, :LANES], x[:, LANES:]], 0)


def rows8(x):
    total = x[:8]
    for at in range(8, x.shape[0], 8):
        total = total + x[at : at + 8]
    return total


def main_kernel(rules, taps, inside, scale,
                q_hbm, k_hbm, v_hbm, c_hbm, *refs):
    smalls, refs = refs[:SMALLS], refs[SMALLS:]
    outputs, held, refs = refs[:7], refs[7 : 7 + SMALLS], refs[7 + SMALLS :]
    mixed_ref, oq_ref, ok_ref, ov_ref, short_ref, gres_ref, gskip_ref = outputs
    dec_ref, res_ref, w_ref, skip_ref, spec_ref, dft_ref, inv_ref, mom_ref, back_ref, lag_ref, far_ref, farb_ref, pick_ref = held
    (xin, xs, cot, sh, gated, gmix, e_ref, h_ref, near, grad, resp, rmom, skp, gs, acc,
                tails, got_tails, heads, got_heads, moms, got_moms, wide_moms, wide_got, parted, got_parts, mine, full,
                in_sem, small_sem, tail_sem, head_sem, mom_send, mom_recv, rs_send, rs_recv, ag_send, ag_recv) = refs
    n = lax.axis_size("ctx")
    me = lax.axis_index("ctx")
    channels, rows = q_hbm.shape
    modes = smalls[0].shape[0]
    blocks = channels // BLOCK
    tiles = BLOCK // LANES
    nodes, turning, reach = rules
    reach = [NODES] + [reach[min(d, n - d) - 1] if n <= 8 else NODES for d in range(1, n)]
    where = [lax.rem(me + d, n) for d in range(n)]

    loads = [pltpu.make_async_copy(ref, xin.at[i], in_sem.at[i]) for i, ref in enumerate((q_hbm, k_hbm, v_hbm, c_hbm))]
    barrier = pltpu.get_barrier_semaphore()
    for d in range(1, n):
        pl.semaphore_signal(barrier, inc=1, device_id={"ctx": where[d]}, device_id_type=MESH)

    for copy in loads:
        copy.start()
    small_loads = [pltpu.make_async_copy(a, b, small_sem.at[i]) for i, (a, b) in enumerate(zip(smalls, held))]
    for copy in small_loads:
        copy.start()

    def remote(src, dst, send_sem, recv_sem, d):
        return pltpu.make_async_remote_copy(
            src_ref=src, dst_ref=dst, send_sem=send_sem, recv_sem=recv_sem,
            device_id={"ctx": where[d]}, device_id_type=MESH)

    def each(body):
        lax.fori_loop(0, blocks, lambda b, c: (body(b), c)[1], 0, unroll=True)

    def cols(b):
        return pl.ds(pl.multiple_of(b * BLOCK, BLOCK), BLOCK)

    def lanes(b, h):
        return pl.ds(pl.multiple_of(b * BLOCK + h * LANES, LANES), LANES)

    eye = (lax.broadcasted_iota(jnp.int32, (rows, rows), 0) == lax.broadcasted_iota(jnp.int32, (rows, rows), 1)).astype(BF16)

    for copy in loads[:3]:
        copy.wait()

    def turn(b):
        for i in range(3):
            x = mm_nt(eye, xin[i, cols(b), :])
            for h in range(tiles):
                xs[i, b * tiles + h, PAD:, :] = x[:, h * LANES : (h + 1) * LANES]
            tails[i, b] = pair(x[rows - 8 :, :]).astype(BF16)

    each(turn)
    pl.semaphore_wait(barrier, n - 1)
    tail = remote(tails, got_tails, tail_sem.at[0], tail_sem.at[1], 1)
    pl.when(me < n - 1)(tail.start)

    @pl.when(me == 0)
    def _():
        got_tails[...] = jnp.zeros_like(got_tails)

    for copy in [loads[3], *small_loads]:
        copy.wait()

    def prepare(b):
        at = cols(b)
        x = mm_nt(eye, xin[3, at, :])
        for h in range(tiles):
            cot[b * tiles + h] = x[:, h * LANES : (h + 1) * LANES]
        dec = dec_ref[:, at]
        gain = res_ref[:, at] * jnp.sqrt(2.0 * dec)
        powers = [jnp.exp(dec * (-x)) for x in nodes]
        half = NODES // 2
        even = [powers[k] + powers[NODES - 1 - k] for k in range(half)]
        odd = [powers[k] - powers[NODES - 1 - k] for k in range(half)]
        terms = []
        for j in range(NODES):
            e = sum(turning[j][k] * (odd if j % 2 else even)[k] for k in range(half))
            e_ref[j, :, at] = e
            terms.append(gain * e)
        h_ref[b] = mm(spec_ref[...], jnp.concatenate(terms, 0).astype(BF16))

    each(prepare)
    def gate(b, h, strips):
        t = b * tiles + h
        hl = slice(h * LANES, (h + 1) * LANES)
        skip_sum = jnp.zeros((8, LANES), F32)
        for r, size in strips:
            short = []
            for i in range(3):
                total = None
                for j in range(taps):
                    term = w_ref[i, j : j + 1, lanes(b, h)] * xs[i, t, PAD + r - j : PAD + r - j + size, :]
                    total = term if total is None else total + term
                sh[i, t, r : r + size, :] = total
                short.append(total)
            x = short[1] * short[2]
            g = cot[t, r : r + size, :] * short[0]
            gated[b, r : r + size, hl] = x.astype(BF16)
            gmix[b, r : r + size, hl] = g.astype(BF16)
            skip_sum = skip_sum + rows8(x * g)
        return skip_sum

    def inner(b):
        for h in range(tiles):
            skp[b * tiles + h] = gate(b, h, [(EDGE, STRIP - EDGE)] + [(r, STRIP) for r in range(STRIP, rows, STRIP)])

    each(inner)
    pl.when(me < n - 1)(tail.wait_send)
    pl.when(me > 0)(tail.wait_recv)

    def edge(b):
        for i in range(3):
            halo = got_tails[i, b].astype(F32)
            for h in range(tiles):
                xs[i, b * tiles + h, :PAD, :] = halo[h * 8 : h * 8 + 8]
        for h in range(tiles):
            t = b * tiles + h
            skp[t] = skp[t] + gate(b, h, [(0, EDGE)])
        s_mom = halves(mm(back_ref[...], gated[b]))
        r_mom = halves(mm(mom_ref[...], gmix[b]))
        rmom[b] = r_mom
        for h in range(tiles):
            hl = slice(h * LANES, (h + 1) * LANES)
            wide_moms[0, :, b * tiles + h, :] = s_mom[:, hl]
            wide_moms[1, :, b * tiles + h, :] = r_mom[:, hl]

    each(edge)
    moms[...] = wide_moms[...].astype(BF16)
    states = []
    for d in range(1, n):
        kind = jnp.where(where[d] > me, 0, 1)
        first = pl.ds(0, reach[d])
        copy = remote(moms.at[kind, first], got_moms.at[d, first], mom_send.at[d], mom_recv.at[d], d)
        copy.start()
        states.append(copy)

    def middle(b):
        z = mm(dft_ref[...], gated[b])
        g = mm(dft_ref[...], gmix[b])
        h = h_ref[b]
        zr, zi = z[:rows], z[rows:]
        gr, gi = g[:rows], g[rows:]
        hr, hi = h[:rows], h[rows:]
        fwd = jnp.concatenate([zr * hr - zi * hi, zr * hi + zi * hr], 0).astype(BF16)
        bwd = jnp.concatenate([gr * hr + gi * hi, gi * hr - gr * hi], 0).astype(BF16)
        lag = jnp.concatenate([gr * zr + gi * zi, gi * zr - gr * zi], 0).astype(BF16)
        near[b] = mm(inv_ref[...], fwd)
        grad[b] = mm(inv_ref[...], bwd)
        moments = halves(mm(lag_ref[...], lag))
        total = jnp.zeros((modes, BLOCK), F32)
        for k in range(NODES):
            total = total + e_ref[k, :, cols(b)] * moments[k : k + 1, :]
        resp[:, cols(b)] = total

    each(middle)
    for copy in states:
        copy.wait()
    for d in range(1, n):
        wide_got[d, : reach[d]] = got_moms[d, : reach[d]].astype(F32)

    def arrive(b):
        at = cols(b)
        dec = dec_ref[:, at]
        root = jnp.sqrt(2.0 * dec)
        one = jnp.exp(-dec)
        chunk = jnp.exp(dec * (-float(rows)))
        es = [e_ref[k, :, at] for k in range(NODES)]

        def spread(rows_of):
            total = es[0] * rows_of[0]
            for e, x in zip(es[1:], rows_of[1:]):
                total = total + e * x
            return total

        def arrived(d, count):
            t = b * tiles
            return spread([jnp.concatenate([wide_got[d, j, pl.ds(t + h, 1), :] for h in range(tiles)], 1) for j in range(count)])

        s = r = jnp.zeros((modes, BLOCK), F32)
        if n <= 8:
            new = [arrived(d, reach[d]) for d in range(1, n)]
            for d in range(n - 1, 0, -1):
                s = jnp.where(me >= d, s * chunk + new[d - 1], s)
            for d in range(1, n):
                r = jnp.where(me < d, r * chunk + new[d - 1], r)
        else:
            s = lax.fori_loop(0, me, lambda i, s: s * chunk + arrived(me - i, NODES), s)
            r = lax.fori_loop(me + 1, n, lambda i, r: r * chunk + arrived(i, NODES), r)
        resp[:, at] = root * (resp[:, at] + one * s * spread([rmom[b, j : j + 1, :] for j in range(NODES)]))
        gain = res_ref[:, at] * root * one
        gain_s, gain_r = gain * s, gain * r
        near[b] = near[b] + mm(far_ref[...], jnp.concatenate([gain_s * e for e in es], 0).astype(BF16))
        grad[b] = grad[b] + mm(farb_ref[...], jnp.concatenate([gain_r * e for e in es], 0).astype(BF16))
        top = [[], [], []]
        for h in range(tiles):
            t = b * tiles + h
            hl = slice(h * LANES, (h + 1) * LANES)
            skip = skip_ref[:, lanes(b, h)]
            qs, ks, vs = (sh[i, t, :8, :] for i in range(3))
            c = cot[t, :8, :]
            back = grad[b, :8, hl] + skip * (c * qs)
            for i, x in enumerate((c * (near[b, :8, hl] + skip * (ks * vs)), back * vs, back * ks)):
                top[i].append(x)
        for i in range(3):
            heads[i, b] = jnp.concatenate(top[i], 0).astype(BF16)

    each(arrive)
    head = remote(heads, got_heads, head_sem.at[0], head_sem.at[1], n - 1)
    pl.when(me > 0)(head.start)

    @pl.when(me == n - 1)
    def _():
        got_heads[...] = jnp.zeros_like(got_heads)


    def last(b):
        at = cols(b)
        for h in range(tiles):
            t = b * tiles + h
            hl = slice(h * LANES, (h + 1) * LANES)
            skip = skip_ref[:, lanes(b, h)]
            sums = [jnp.zeros((8, LANES), F32)] * (3 * taps)
            out = []
            for r0 in range(0, rows, STRIP):
                rr = slice(r0, r0 + STRIP)
                qs, ks, vs = (sh[i, t, rr, :] for i in range(3))
                c = cot[t, rr, :]
                mix = near[b, rr, hl] + skip * (ks * vs)
                back = grad[b, rr, hl] + skip * (c * qs)
                out.append(qs * mix)
                grads = (c * mix, back * vs, back * ks)
                for i in range(3):
                    gs[i, t, rr, :] = grads[i]
                    for j in range(taps):
                        shifted = xs[i, t, PAD + r0 - j : PAD + r0 - j + STRIP, :]
                        sums[i * taps + j] = sums[i * taps + j] + rows8(grads[i] * shifted)
            mixed_ref[lanes(b, h), :] = jnp.concatenate(out, 0).T.astype(BF16)
            for a in range(3 * taps):
                acc[a * 8 : a * 8 + 8, hl] = sums[a]
            acc[3 * taps * 8 :, hl] = skp[t]
        total = jnp.concatenate([resp[:, at], mm(pick_ref[...], acc[...].astype(BF16))], 0)
        if inside:
            parted[b] = pair(total).astype(BF16)
        else:
            gres_ref[:, at] = total[:modes]
            for i in range(3):
                short_ref[i, :, at] = total[modes + 8 * i : modes + 8 * i + taps]
            gskip_ref[:, at] = total[modes + 7 : modes + 8]

    pieces = []
    if inside:
        for d in range(1, n):
            last(where[d])
            copy = remote(parted.at[where[d]], got_parts.at[d], rs_send.at[d], rs_recv.at[d], d)
            copy.start()
            pieces.append(copy)
        last(me)
    else:
        each(last)

    outs = (oq_ref, ok_ref, ov_ref)

    def final(b):
        at = cols(b)
        for i in range(3):
            halo = got_heads[i, b].astype(F32)
            for h in range(tiles):
                gs[i, b * tiles + h, rows:, :] = halo[h * 8 : h * 8 + 8]
        for h in range(tiles):
            t = b * tiles + h
            for i in range(3):
                out = []
                for r in range(0, rows, STRIP):
                    total = None
                    for j in range(taps):
                        term = w_ref[i, j : j + 1, lanes(b, h)] * gs[i, t, r + j : r + j + STRIP, :]
                        total = term if total is None else total + term
                    out.append(total)
                outs[i][lanes(b, h), :] = jnp.concatenate(out, 0).T.astype(BF16)

    if inside:
        total = parted[me].astype(F32)
        for d in range(1, n):
            pieces[d - 1].wait()
            total = total + got_parts[d].astype(F32)
        mine[...] = (total * scale).astype(BF16)
        pieces = []
        for d in range(1, n):
            copy = remote(mine, full.at[d], ag_send.at[d], ag_recv.at[d], d)
            copy.start()
            pieces.append(copy)
        full[0] = mine[...]
    pl.when(me > 0)(head.wait_send)
    pl.when(me < n - 1)(head.wait_recv)
    each(final)
    if inside:
        for copy in pieces:
            copy.wait()
        height = modes + 24
        for p in range(n):
            value = full[lax.rem(me - p + n, n)].astype(F32)
            for h in range(tiles):
                x = value[h * height : (h + 1) * height]
                hl = slice(p * BLOCK + h * LANES, p * BLOCK + (h + 1) * LANES)
                gres_ref[:, hl] = x[:modes]
                for i in range(3):
                    short_ref[i, :, hl] = x[modes + 8 * i : modes + 8 * i + taps]
                gskip_ref[:, hl] = x[modes + 7 : modes + 8]


def output_kernel(*refs):
    count = (len(refs) - 1) // 2
    sems = refs[-1]
    copies = [pltpu.make_async_copy(refs[i], refs[count + i], sems.at[i]) for i in range(count)]
    for copy in copies:
        copy.start()
    for copy in copies:
        copy.wait()


def per_device(queries, key_signal, value_signal, cotangent, short_weight, residues, decay_rates, skip_gain):
    channels, rows = queries.shape
    taps = short_weight.shape[1]
    modes = residues.shape[1]
    n = lax.axis_size("ctx")
    rules, tab = tables(rows, taps, modes)
    blocks, count = channels // BLOCK, channels // LANES
    inside = channels // n == BLOCK
    scale = 1.0 / math.sqrt(rows * n)
    height = 2 * (modes + 24)
    dma = pltpu.SemaphoreType.DMA

    def shape(*dims, kind=F32):
        return jax.ShapeDtypeStruct(dims, kind)

    vmem = pl.BlockSpec(memory_space=pltpu.VMEM)
    hbm = pl.BlockSpec(memory_space=pl.ANY)
    names = ("spec", "dft", "inv", "mom", "mom_back", "lag", "far", "far_back", "pick")
    args = [decay_rates.T, residues.T, short_weight, skip_gain[None, :]] + [jnp.asarray(tab[name]) for name in names]
    owners = n if inside else 1
    mixed, gq, gk, gv, short, gres, gskip = pl.pallas_call(
        functools.partial(main_kernel, rules, taps, inside, scale),
        in_specs=[hbm] * (4 + SMALLS),
        out_specs=[vmem] * 7,
        out_shape=[pltpu.VMEM((channels, rows), BF16)] * 4 + [pltpu.VMEM((3, taps, channels), F32), pltpu.VMEM((modes, channels), F32), pltpu.VMEM((1, channels), F32)],
        scratch_shapes=[pltpu.VMEM(x.shape, x.dtype) for x in args]
        + [
            pltpu.VMEM((4, channels, rows), BF16),
            pltpu.VMEM((3, count, rows + PAD, LANES), F32),
            pltpu.VMEM((count, rows, LANES), F32),
            pltpu.VMEM((3, count, rows, LANES), F32),
            pltpu.VMEM((blocks, rows, BLOCK), BF16),
            pltpu.VMEM((blocks, rows, BLOCK), BF16),
            pltpu.VMEM((NODES, modes, channels), F32),
            pltpu.VMEM((blocks, 2 * rows, BLOCK), F32),
            pltpu.VMEM((blocks, rows, BLOCK), F32),
            pltpu.VMEM((blocks, rows, BLOCK), F32),
            pltpu.VMEM((modes, channels), F32),
            pltpu.VMEM((blocks, NODES, BLOCK), F32),
            pltpu.VMEM((count, 8, LANES), F32),
            pltpu.VMEM((3, count, rows + PAD, LANES), F32),
            pltpu.VMEM((8 * (3 * taps + 1), BLOCK), F32),
            pltpu.VMEM((3, blocks, 16, LANES), BF16),
            pltpu.VMEM((3, blocks, 16, LANES), BF16),
            pltpu.VMEM((3, blocks, 16, LANES), BF16),
            pltpu.VMEM((3, blocks, 16, LANES), BF16),
            pltpu.VMEM((2, NODES, count, LANES), BF16),
            pltpu.VMEM((n, NODES, count, LANES), BF16),
            pltpu.VMEM((2, NODES, count, LANES), F32),
            pltpu.VMEM((n, NODES, count, LANES), F32),
            pltpu.VMEM((owners, height, LANES), BF16),
            pltpu.VMEM((owners, height, LANES), BF16),
            pltpu.VMEM((height, LANES), BF16),
            pltpu.VMEM((owners, height, LANES), BF16),
            dma((4,)), dma((SMALLS,)), dma((2,)), dma((2,)),
            dma((n,)), dma((n,)), dma((owners,)), dma((owners,)), dma((owners,)), dma((owners,)),
        ],
        compiler_params=pltpu.CompilerParams(collective_id=0, has_side_effects=True, vmem_limit_bytes=60 * 1024 * 1024),
        cost_estimate=pl.CostEstimate(flops=4 * 10**9, bytes_accessed=5 * 10**6, transcendentals=3 * 10**5),
        name="hyena",
    )(queries, key_signal, value_signal, cotangent, *args)
    if not inside:
        short, gres, gskip = (lax.psum(x, "ctx") * scale for x in (short, gres, gskip))
    else:
        values = (mixed, gq, gk, gv, short, gres, gskip)
        mixed, gq, gk, gv, short, gres, gskip = pl.pallas_call(
            output_kernel,
            in_specs=[vmem] * 7,
            out_specs=[hbm] * 7,
            out_shape=[shape(*x.shape, kind=x.dtype) for x in values],
            scratch_shapes=[dma((7,))],
            name="output",
        )(*[pltpu.with_memory_space_constraint(x, pltpu.VMEM) for x in values])
    return mixed, gq, gk, gv, short, gres.T, gskip[0]


def solution(mesh):
    signal = P("tp", "ctx")
    in_specs = (signal,) * 4 + (P(None, None, "tp"), P("tp", None), P("tp", None), P("tp"))
    out_specs = (signal,) * 4 + (P(None, None, "tp"), P("tp", None), P("tp"))
    return jax.shard_map(
        per_device, mesh=mesh, in_specs=in_specs, out_specs=out_specs, check_vma=False
    )
```

```python
import functools
import math

import jax
import jax.numpy as jnp
import ml_dtypes
import numpy as np
from jax import lax
from jax.experimental import pallas as pl
from jax.experimental.pallas import tpu as pltpu
from jax.sharding import PartitionSpec as P

F32 = jnp.float32
BF16 = jnp.bfloat16
NODES = 8
LANES = 128
SMALLS = 13
MAX_DECAY = 0.03
BLOCK = 256
STRIP = 64
EDGE = 16
PAD = 8
MESH = pl.DeviceIdType.MESH


def two(table):
    high = table.astype(ml_dtypes.bfloat16)
    low = (table - high.astype(np.float64)).astype(ml_dtypes.bfloat16)
    return high, low


@functools.lru_cache(None)
def tables(rows, taps, modes):
    top = rows - 1
    points = -np.cos((2 * np.arange(NODES) + 1) * math.pi / (2 * NODES))
    order = np.arange(NODES)

    def cheb(y):
        return np.cos(order[:, None] * np.arccos(y)[None, :])

    nodes = top / 2 * (1 + points)
    turn = cheb(points) * (2 - (order == 0))[:, None] / NODES
    spots = np.arange(rows, dtype=np.float64)
    basis = cheb(spots / (top / 2) - 1)
    decays = np.linspace(0, MAX_DECAY, 401)
    shares = np.abs(turn @ np.exp(-nodes[:, None] * decays))
    reach = []
    for distance in range(1, 8):
        left = np.cumsum((shares * np.exp(-decays * rows * (distance - 1)))[::-1], 0)[::-1].max(1)
        reach.append(NODES if distance == 1 else int(next(j for j in range(NODES + 1) if j == NODES or left[j] < 1e-5)))
    back = basis[:, ::-1]
    omega = 2 * math.pi * (np.arange(rows) + 0.5) / (2 * rows)
    angle = spots[:, None] * omega[None, :]
    dft = np.concatenate([np.cos(angle), -np.sin(angle)], 1)
    inv = dft / rows

    def wide(table):
        return two(np.repeat(table, modes, 1))[0]

    out = {}
    out["spec"] = wide(dft.T @ basis.T)
    out["dft"] = two(dft.T)[0]
    out["inv"] = two(inv)[0]
    out["mom"] = np.concatenate(two(basis), 0)
    out["mom_back"] = np.concatenate(two(back), 0)
    out["lag"] = np.concatenate(two(basis @ inv), 0)
    out["far"] = wide(basis.T)
    out["far_back"] = wide(back.T)
    count = 3 * taps + 1
    pick = np.zeros((24, count * 8))
    for i in range(3):
        for j in range(taps):
            at = i * taps + j
            pick[i * 8 + j, at * 8 : at * 8 + 8] = 1
    pick[7, (count - 1) * 8 :] = 1
    out["pick"] = two(pick)[0]
    return (nodes.tolist(), turn.tolist(), reach), out


def mm(a, b):
    return lax.dot_general(a, b, (((1,), (0,)), ((), ())), preferred_element_type=F32)


def mm_nt(a, b):
    return lax.dot_general(a, b, (((1,), (1,)), ((), ())), preferred_element_type=F32)


def halves(x):
    return x[:NODES] + x[NODES:]


def pair(x):
    return jnp.concatenate([x[:, :LANES], x[:, LANES:]], 0)


def rows8(x):
    total = x[:8]
    for at in range(8, x.shape[0], 8):
        total = total + x[at : at + 8]
    return total


def main_kernel(rules, taps, inside, scale,
                q_hbm, k_hbm, v_hbm, c_hbm, *refs):
    smalls, refs = refs[:SMALLS], refs[SMALLS:]
    outputs, held, refs = refs[:7], refs[7 : 7 + SMALLS], refs[7 + SMALLS :]
    mixed_ref, oq_ref, ok_ref, ov_ref, short_ref, gres_ref, gskip_ref = outputs
    dec_ref, res_ref, w_ref, skip_ref, spec_ref, dft_ref, inv_ref, mom_ref, back_ref, lag_ref, far_ref, farb_ref, pick_ref = held
    (xin, xs, cot, sh, gated, gmix, e_ref, h_ref, near, grad, resp, rmom, skp, gs, acc,
                tails, got_tails, heads, got_heads, moms, got_moms, wide_moms, wide_got, carried, power, parted, got_parts, mine, full,
                in_sem, small_sem, tail_sem, head_sem, mom_send, mom_recv, rs_send, rs_recv, ag_send, ag_recv) = refs
    n = lax.axis_size("ctx")
    me = lax.axis_index("ctx")
    channels, rows = q_hbm.shape
    modes = smalls[0].shape[0]
    blocks = channels // BLOCK
    tiles = BLOCK // LANES
    nodes, turning, reach = rules
    reach = [NODES] + [reach[min(d, n - d) - 1] if n <= 8 else NODES for d in range(1, n)]
    few = n <= 8
    where = [lax.rem(me + d, n) for d in range(n)]

    loads = [pltpu.make_async_copy(ref, xin.at[i], in_sem.at[i]) for i, ref in enumerate((q_hbm, k_hbm, v_hbm, c_hbm))]
    barrier = pltpu.get_barrier_semaphore()
    for d in range(1, n):
        pl.semaphore_signal(barrier, inc=1, device_id={"ctx": where[d]}, device_id_type=MESH)

    for copy in loads:
        copy.start()
    small_loads = [pltpu.make_async_copy(a, b, small_sem.at[i]) for i, (a, b) in enumerate(zip(smalls, held))]
    for copy in small_loads:
        copy.start()

    def remote(src, dst, send_sem, recv_sem, d):
        return pltpu.make_async_remote_copy(
            src_ref=src, dst_ref=dst, send_sem=send_sem, recv_sem=recv_sem,
            device_id={"ctx": where[d]}, device_id_type=MESH)

    def each(body):
        lax.fori_loop(0, blocks, lambda b, c: (body(b), c)[1], 0, unroll=True)

    def cols(b):
        return pl.ds(pl.multiple_of(b * BLOCK, BLOCK), BLOCK)

    def lanes(b, h):
        return pl.ds(pl.multiple_of(b * BLOCK + h * LANES, LANES), LANES)

    eye = (lax.broadcasted_iota(jnp.int32, (rows, rows), 0) == lax.broadcasted_iota(jnp.int32, (rows, rows), 1)).astype(BF16)

    def turn(i, b):
        x = mm_nt(eye, xin[i, cols(b), :])
        for h in range(tiles):
            xs[i, b * tiles + h, PAD:, :] = x[:, h * LANES : (h + 1) * LANES]
        tails[i, b] = pair(x[rows - 8 :, :]).astype(BF16)

    halos = [remote(tails.at[i], got_tails.at[i], tail_sem.at[0, i], tail_sem.at[1, i], 1) for i in range(3)]
    for i in range(3):
        loads[i].wait()
        each(functools.partial(turn, i))
        if i == 0:
            pl.semaphore_wait(barrier, n - 1)
        pl.when(me < n - 1)(halos[i].start)

    @pl.when(me == 0)
    def _():
        got_tails[...] = jnp.zeros_like(got_tails)

    for copy in [loads[3], *small_loads]:
        copy.wait()

    def prepare(b):
        at = cols(b)
        x = mm_nt(eye, xin[3, at, :])
        for h in range(tiles):
            cot[b * tiles + h] = x[:, h * LANES : (h + 1) * LANES]
    each(prepare)
    def gate(b, h, strips):
        t = b * tiles + h
        hl = slice(h * LANES, (h + 1) * LANES)
        skip_sum = jnp.zeros((8, LANES), F32)
        for r, size in strips:
            short = []
            for i in range(3):
                total = None
                for j in range(taps):
                    term = w_ref[i, j : j + 1, lanes(b, h)] * xs[i, t, PAD + r - j : PAD + r - j + size, :]
                    total = term if total is None else total + term
                sh[i, t, r : r + size, :] = total
                short.append(total)
            x = short[1] * short[2]
            g = cot[t, r : r + size, :] * short[0]
            gated[b, r : r + size, hl] = x.astype(BF16)
            gmix[b, r : r + size, hl] = g.astype(BF16)
            skip_sum = skip_sum + rows8(x * g)
        return skip_sum

    def inner(b):
        for h in range(tiles):
            skp[b * tiles + h] = gate(b, h, [(EDGE, STRIP - EDGE)] + [(r, STRIP) for r in range(STRIP, rows, STRIP)])

    each(inner)
    for halo in halos:
        pl.when(me < n - 1)(halo.wait_send)
        pl.when(me > 0)(halo.wait_recv)

    def edge(b):
        for i in range(3):
            halo = got_tails[i, b].astype(F32)
            for h in range(tiles):
                xs[i, b * tiles + h, :PAD, :] = halo[h * 8 : h * 8 + 8]
        for h in range(tiles):
            t = b * tiles + h
            skp[t] = skp[t] + gate(b, h, [(0, EDGE)])
        s_mom = halves(mm(back_ref[...], gated[b]))
        r_mom = halves(mm(mom_ref[...], gmix[b]))
        rmom[b] = r_mom
        for h in range(tiles):
            hl = slice(h * LANES, (h + 1) * LANES)
            wide_moms[0, :, b * tiles + h, :] = s_mom[:, hl]
            wide_moms[1, :, b * tiles + h, :] = r_mom[:, hl]

    each(edge)
    moms[...] = wide_moms[...].astype(BF16)
    states = []
    for d in range(1, n):
        kind = jnp.where(where[d] > me, 0, 1)
        first = pl.ds(0, reach[d])
        copy = remote(moms.at[kind, first], got_moms.at[d, first], mom_send.at[d], mom_recv.at[d], d)
        copy.start()
        states.append(copy)

    def filters(b):
        at = cols(b)
        dec = dec_ref[:, at]
        gain = res_ref[:, at] * jnp.sqrt(2.0 * dec)
        if few:
            carried[:, :, at] = jnp.zeros((2, modes, BLOCK), F32)
            chunk = jnp.exp(dec * (-float(rows)))
            total = jnp.ones_like(dec)
            for d in range(n - 1):
                power[d, :, at] = total
                total = total * chunk
        powers = [jnp.exp(dec * (-x)) for x in nodes]
        half = NODES // 2
        even = [powers[k] + powers[NODES - 1 - k] for k in range(half)]
        odd = [powers[k] - powers[NODES - 1 - k] for k in range(half)]
        terms = []
        for j in range(NODES):
            e = sum(turning[j][k] * (odd if j % 2 else even)[k] for k in range(half))
            e_ref[j, :, at] = e
            terms.append(gain * e)
        h_ref[b] = mm(spec_ref[...], jnp.concatenate(terms, 0).astype(BF16))

    each(filters)

    def middle(b):
        z = mm(dft_ref[...], gated[b])
        g = mm(dft_ref[...], gmix[b])
        h = h_ref[b]
        zr, zi = z[:rows], z[rows:]
        gr, gi = g[:rows], g[rows:]
        hr, hi = h[:rows], h[rows:]
        fwd = jnp.concatenate([zr * hr - zi * hi, zr * hi + zi * hr], 0).astype(BF16)
        bwd = jnp.concatenate([gr * hr + gi * hi, gi * hr - gr * hi], 0).astype(BF16)
        lag = jnp.concatenate([gr * zr + gi * zi, gi * zr - gr * zi], 0).astype(BF16)
        near[b] = mm(inv_ref[...], fwd)
        grad[b] = mm(inv_ref[...], bwd)
        moments = halves(mm(lag_ref[...], lag))
        total = jnp.zeros((modes, BLOCK), F32)
        for k in range(NODES):
            total = total + e_ref[k, :, cols(b)] * moments[k : k + 1, :]
        resp[:, cols(b)] = total

    each(middle)
    def arrived(b, d, count):
        total = None
        for j in range(count):
            x = jnp.concatenate([wide_got[d, j, pl.ds(b * tiles + h, 1), :] for h in range(tiles)], 1)
            term = e_ref[j, :, cols(b)] * x
            total = term if total is None else total + term
        return total

    def collect(d):
        states[d - 1].wait()
        wide_got[d, : reach[d]] = got_moms[d, : reach[d]].astype(F32)
        kind = jnp.where(me >= d, 0, 1)
        steps = jnp.where(me >= d, d, n - d) - 1

        def add(b):
            at = cols(b)
            carried[kind, :, at] = carried[kind, :, at] + power[steps, :, at] * arrived(b, d, reach[d])

        each(add)

    if few:
        for d in sorted(range(1, n), key=lambda d: min(d, n - d)):
            collect(d)
    else:
        for d in range(1, n):
            states[d - 1].wait()
            wide_got[d] = got_moms[d].astype(F32)

    def arrive(b):
        at = cols(b)
        dec = dec_ref[:, at]
        root = jnp.sqrt(2.0 * dec)
        one = jnp.exp(-dec)
        chunk = jnp.exp(dec * (-float(rows)))
        es = [e_ref[k, :, at] for k in range(NODES)]

        def spread(rows_of):
            total = es[0] * rows_of[0]
            for e, x in zip(es[1:], rows_of[1:]):
                total = total + e * x
            return total

        if few:
            s, r = carried[0, :, at], carried[1, :, at]
        else:
            s = r = jnp.zeros((modes, BLOCK), F32)
            s = lax.fori_loop(0, me, lambda i, s: s * chunk + arrived(b, me - i, NODES), s)
            r = lax.fori_loop(me + 1, n, lambda i, r: r * chunk + arrived(b, i, NODES), r)
        resp[:, at] = root * (resp[:, at] + one * s * spread([rmom[b, j : j + 1, :] for j in range(NODES)]))
        gain = res_ref[:, at] * root * one
        gain_s, gain_r = gain * s, gain * r
        near[b] = near[b] + mm(far_ref[...], jnp.concatenate([gain_s * e for e in es], 0).astype(BF16))
        grad[b] = grad[b] + mm(farb_ref[...], jnp.concatenate([gain_r * e for e in es], 0).astype(BF16))
        top = [[], [], []]
        for h in range(tiles):
            t = b * tiles + h
            hl = slice(h * LANES, (h + 1) * LANES)
            skip = skip_ref[:, lanes(b, h)]
            qs, ks, vs = (sh[i, t, :8, :] for i in range(3))
            c = cot[t, :8, :]
            back = grad[b, :8, hl] + skip * (c * qs)
            for i, x in enumerate((c * (near[b, :8, hl] + skip * (ks * vs)), back * vs, back * ks)):
                top[i].append(x)
        for i in range(3):
            heads[i, b] = jnp.concatenate(top[i], 0).astype(BF16)

    each(arrive)
    head = remote(heads, got_heads, head_sem.at[0], head_sem.at[1], n - 1)
    pl.when(me > 0)(head.start)

    @pl.when(me == n - 1)
    def _():
        got_heads[...] = jnp.zeros_like(got_heads)


    def last(b):
        at = cols(b)
        for h in range(tiles):
            t = b * tiles + h
            hl = slice(h * LANES, (h + 1) * LANES)
            skip = skip_ref[:, lanes(b, h)]
            sums = [jnp.zeros((8, LANES), F32)] * (3 * taps)
            for r0 in range(0, rows, STRIP):
                rr = slice(r0, r0 + STRIP)
                qs, ks, vs = (sh[i, t, rr, :] for i in range(3))
                c = cot[t, rr, :]
                mix = near[b, rr, hl] + skip * (ks * vs)
                back = grad[b, rr, hl] + skip * (c * qs)
                near[b, rr, hl] = qs * mix
                grads = (c * mix, back * vs, back * ks)
                for i in range(3):
                    gs[i, t, rr, :] = grads[i]
                    for j in range(taps):
                        shifted = xs[i, t, PAD + r0 - j : PAD + r0 - j + STRIP, :]
                        sums[i * taps + j] = sums[i * taps + j] + rows8(grads[i] * shifted)
            for a in range(3 * taps):
                acc[a * 8 : a * 8 + 8, hl] = sums[a]
            acc[3 * taps * 8 :, hl] = skp[t]
        total = jnp.concatenate([resp[:, at], mm(pick_ref[...], acc[...].astype(BF16))], 0)
        if inside:
            parted[b] = pair(total).astype(BF16)
        else:
            gres_ref[:, at] = total[:modes]
            for i in range(3):
                short_ref[i, :, at] = total[modes + 8 * i : modes + 8 * i + taps]
            gskip_ref[:, at] = total[modes + 7 : modes + 8]

    pieces = []
    if inside:
        for d in range(1, n):
            last(where[d])
            copy = remote(parted.at[where[d]], got_parts.at[d], rs_send.at[d], rs_recv.at[d], d)
            copy.start()
            pieces.append(copy)
        last(me)
    else:
        each(last)

    outs = (oq_ref, ok_ref, ov_ref)

    def final(b):
        at = cols(b)
        for i in range(3):
            halo = got_heads[i, b].astype(F32)
            for h in range(tiles):
                gs[i, b * tiles + h, rows:, :] = halo[h * 8 : h * 8 + 8]
        for h in range(tiles):
            t = b * tiles + h
            mixed_ref[lanes(b, h), :] = near[b, :, h * LANES : (h + 1) * LANES].T.astype(BF16)
            for i in range(3):
                out = []
                for r in range(0, rows, STRIP):
                    total = None
                    for j in range(taps):
                        term = w_ref[i, j : j + 1, lanes(b, h)] * gs[i, t, r + j : r + j + STRIP, :]
                        total = term if total is None else total + term
                    out.append(total)
                outs[i][lanes(b, h), :] = jnp.concatenate(out, 0).T.astype(BF16)

    if inside:
        total = parted[me].astype(F32)
        for d in range(1, n):
            pieces[d - 1].wait()
            total = total + got_parts[d].astype(F32)
        mine[...] = (total * scale).astype(BF16)
        pieces = []
        for d in range(1, n):
            copy = remote(mine, full.at[d], ag_send.at[d], ag_recv.at[d], d)
            copy.start()
            pieces.append(copy)
        full[0] = mine[...]
    pl.when(me > 0)(head.wait_send)
    pl.when(me < n - 1)(head.wait_recv)
    each(final)
    def unpack(slot, p):
        value = full[slot].astype(F32)
        for h in range(tiles):
            x, hl = value[h * height : (h + 1) * height], lanes(p, h)
            gres_ref[:, hl] = x[:modes]
            for i in range(3):
                short_ref[i, :, hl] = x[modes + 8 * i : modes + 8 * i + taps]
            gskip_ref[:, hl] = x[modes + 7 : modes + 8]

    if inside:
        height = modes + 24
        unpack(0, me)
        for d in range(1, n):
            pieces[d - 1].wait()
            unpack(d, where[n - d])


def output_kernel(*refs):
    count = (len(refs) - 1) // 2
    sems = refs[-1]
    copies = [pltpu.make_async_copy(refs[i], refs[count + i], sems.at[i]) for i in range(count)]
    for copy in copies:
        copy.start()
    for copy in copies:
        copy.wait()


def per_device(queries, key_signal, value_signal, cotangent, short_weight, residues, decay_rates, skip_gain):
    channels, rows = queries.shape
    taps = short_weight.shape[1]
    modes = residues.shape[1]
    n = lax.axis_size("ctx")
    rules, tab = tables(rows, taps, modes)
    blocks, count = channels // BLOCK, channels // LANES
    inside = channels // n == BLOCK
    scale = 1.0 / math.sqrt(rows * n)
    height = 2 * (modes + 24)
    dma = pltpu.SemaphoreType.DMA

    def shape(*dims, kind=F32):
        return jax.ShapeDtypeStruct(dims, kind)

    vmem = pl.BlockSpec(memory_space=pltpu.VMEM)
    hbm = pl.BlockSpec(memory_space=pl.ANY)
    names = ("spec", "dft", "inv", "mom", "mom_back", "lag", "far", "far_back", "pick")
    args = [decay_rates.T, residues.T, short_weight, skip_gain[None, :]] + [jnp.asarray(tab[name]) for name in names]
    owners = n if inside else 1
    mixed, gq, gk, gv, short, gres, gskip = pl.pallas_call(
        functools.partial(main_kernel, rules, taps, inside, scale),
        in_specs=[hbm] * (4 + SMALLS),
        out_specs=[vmem] * 7,
        out_shape=[pltpu.VMEM((channels, rows), BF16)] * 4 + [pltpu.VMEM((3, taps, channels), F32), pltpu.VMEM((modes, channels), F32), pltpu.VMEM((1, channels), F32)],
        scratch_shapes=[pltpu.VMEM(x.shape, x.dtype) for x in args]
        + [
            pltpu.VMEM((4, channels, rows), BF16),
            pltpu.VMEM((3, count, rows + PAD, LANES), F32),
            pltpu.VMEM((count, rows, LANES), F32),
            pltpu.VMEM((3, count, rows, LANES), F32),
            pltpu.VMEM((blocks, rows, BLOCK), BF16),
            pltpu.VMEM((blocks, rows, BLOCK), BF16),
            pltpu.VMEM((NODES, modes, channels), F32),
            pltpu.VMEM((blocks, 2 * rows, BLOCK), F32),
            pltpu.VMEM((blocks, rows, BLOCK), F32),
            pltpu.VMEM((blocks, rows, BLOCK), F32),
            pltpu.VMEM((modes, channels), F32),
            pltpu.VMEM((blocks, NODES, BLOCK), F32),
            pltpu.VMEM((count, 8, LANES), F32),
            pltpu.VMEM((3, count, rows + PAD, LANES), F32),
            pltpu.VMEM((8 * (3 * taps + 1), BLOCK), F32),
            pltpu.VMEM((3, blocks, 16, LANES), BF16),
            pltpu.VMEM((3, blocks, 16, LANES), BF16),
            pltpu.VMEM((3, blocks, 16, LANES), BF16),
            pltpu.VMEM((3, blocks, 16, LANES), BF16),
            pltpu.VMEM((2, NODES, count, LANES), BF16),
            pltpu.VMEM((n, NODES, count, LANES), BF16),
            pltpu.VMEM((2, NODES, count, LANES), F32),
            pltpu.VMEM((n, NODES, count, LANES), F32),
            pltpu.VMEM((2, modes, channels), F32),
            pltpu.VMEM((min(n, 8), modes, channels), F32),
            pltpu.VMEM((owners, height, LANES), BF16),
            pltpu.VMEM((owners, height, LANES), BF16),
            pltpu.VMEM((height, LANES), BF16),
            pltpu.VMEM((owners, height, LANES), BF16),
            dma((4,)), dma((SMALLS,)), dma((2, 3)), dma((2,)),
            dma((n,)), dma((n,)), dma((owners,)), dma((owners,)), dma((owners,)), dma((owners,)),
        ],
        compiler_params=pltpu.CompilerParams(collective_id=0, has_side_effects=True, vmem_limit_bytes=60 * 1024 * 1024),
        cost_estimate=pl.CostEstimate(flops=4 * 10**9, bytes_accessed=5 * 10**6, transcendentals=3 * 10**5),
        name="hyena",
    )(queries, key_signal, value_signal, cotangent, *args)
    if not inside:
        short, gres, gskip = (lax.psum(x, "ctx") * scale for x in (short, gres, gskip))
    else:
        values = (mixed, gq, gk, gv, short, gres, gskip)
        mixed, gq, gk, gv, short, gres, gskip = pl.pallas_call(
            output_kernel,
            in_specs=[vmem] * 7,
            out_specs=[hbm] * 7,
            out_shape=[shape(*x.shape, kind=x.dtype) for x in values],
            scratch_shapes=[dma((7,))],
            name="output",
        )(*[pltpu.with_memory_space_constraint(x, pltpu.VMEM) for x in values])
    return mixed, gq, gk, gv, short, gres.T, gskip[0]


def solution(mesh):
    signal = P("tp", "ctx")
    in_specs = (signal,) * 4 + (P(None, None, "tp"), P("tp", None), P("tp", None), P("tp"))
    out_specs = (signal,) * 4 + (P(None, None, "tp"), P("tp", None), P("tp"))
    return jax.shard_map(
        per_device, mesh=mesh, in_specs=in_specs, out_specs=out_specs, check_vma=False
    )
```

```python
import functools
import math

import jax
import jax.numpy as jnp
import ml_dtypes
import numpy as np
from jax import lax
from jax.experimental import pallas as pl
from jax.experimental.pallas import tpu as pltpu
from jax.sharding import PartitionSpec as P

F32 = jnp.float32
BF16 = jnp.bfloat16
NODES = 8
LANES = 128
SMALLS = 13
MAX_DECAY = 0.03
BLOCK = 256
STRIP = 64
EDGE = 16
PAD = 8
MESH = pl.DeviceIdType.MESH


def two(table):
    high = table.astype(ml_dtypes.bfloat16)
    low = (table - high.astype(np.float64)).astype(ml_dtypes.bfloat16)
    return high, low


@functools.lru_cache(None)
def tables(rows, taps, modes):
    top = rows - 1
    points = -np.cos((2 * np.arange(NODES) + 1) * math.pi / (2 * NODES))
    order = np.arange(NODES)

    def cheb(y):
        return np.cos(order[:, None] * np.arccos(y)[None, :])

    nodes = top / 2 * (1 + points)
    turn = cheb(points) * (2 - (order == 0))[:, None] / NODES
    spots = np.arange(rows, dtype=np.float64)
    basis = cheb(spots / (top / 2) - 1)
    decays = np.linspace(0, MAX_DECAY, 401)
    shares = np.abs(turn @ np.exp(-nodes[:, None] * decays))
    reach = []
    for distance in range(1, 8):
        left = np.cumsum((shares * np.exp(-decays * rows * (distance - 1)))[::-1], 0)[::-1].max(1)
        reach.append(NODES if distance == 1 else int(next(j for j in range(NODES + 1) if j == NODES or left[j] < 1e-5)))
    back = basis[:, ::-1]
    omega = 2 * math.pi * (np.arange(rows) + 0.5) / (2 * rows)
    angle = spots[:, None] * omega[None, :]
    dft = np.concatenate([np.cos(angle), -np.sin(angle)], 1)
    inv = dft / rows

    def wide(table):
        return two(np.repeat(table, modes, 1))[0]

    out = {}
    out["spec"] = wide(dft.T @ basis.T)
    out["dft"] = two(dft.T)[0]
    out["inv"] = two(inv)[0]
    out["mom"] = np.concatenate(two(basis), 0)
    out["mom_back"] = np.concatenate(two(back), 0)
    out["lag"] = np.concatenate(two(basis @ inv), 0)
    out["far"] = wide(basis.T)
    out["far_back"] = wide(back.T)
    count = 3 * taps + 1
    pick = np.zeros((24, count * 8))
    for i in range(3):
        for j in range(taps):
            at = i * taps + j
            pick[i * 8 + j, at * 8 : at * 8 + 8] = 1
    pick[7, (count - 1) * 8 :] = 1
    out["pick"] = two(pick)[0]
    return (nodes.tolist(), turn.tolist(), reach), out


def mm(a, b):
    return lax.dot_general(a, b, (((1,), (0,)), ((), ())), preferred_element_type=F32)


def mm_nt(a, b):
    return lax.dot_general(a, b, (((1,), (1,)), ((), ())), preferred_element_type=F32)


def halves(x):
    return x[:NODES] + x[NODES:]


def pair(x):
    return jnp.concatenate([x[:, :LANES], x[:, LANES:]], 0)


def rows8(x):
    total = x[:8]
    for at in range(8, x.shape[0], 8):
        total = total + x[at : at + 8]
    return total


def main_kernel(rules, taps, inside, scale,
                q_hbm, k_hbm, v_hbm, c_hbm, *refs):
    smalls, refs = refs[:SMALLS], refs[SMALLS:]
    outputs, held, refs = refs[:7], refs[7 : 7 + SMALLS], refs[7 + SMALLS :]
    mixed_ref, oq_ref, ok_ref, ov_ref, short_ref, gres_ref, gskip_ref = outputs
    dec_ref, res_ref, w_ref, skip_ref, spec_ref, dft_ref, inv_ref, mom_ref, back_ref, lag_ref, far_ref, farb_ref, pick_ref = held
    (xin, xs, cot, sh, gated, gmix, e_ref, h_ref, near, grad, resp, rmom, skp, gs, acc,
                tails, got_tails, heads, got_heads, moms, got_moms, wide_moms, wide_got, carried, power, parted, got_parts, mine, full,
                in_sem, small_sem, tail_sem, head_sem, mom_send, mom_recv, rs_send, rs_recv, ag_send, ag_recv) = refs
    n = lax.axis_size("ctx")
    me = lax.axis_index("ctx")
    channels, rows = q_hbm.shape
    modes = smalls[0].shape[0]
    blocks = channels // BLOCK
    tiles = BLOCK // LANES
    nodes, turning, reach = rules
    reach = [NODES] + [reach[min(d, n - d) - 1] if n <= 8 else NODES for d in range(1, n)]
    few = n <= 8
    where = [lax.rem(me + d, n) for d in range(n)]

    loads = [pltpu.make_async_copy(ref, xin.at[i], in_sem.at[i]) for i, ref in enumerate((q_hbm, k_hbm, v_hbm, c_hbm))]
    barrier = pltpu.get_barrier_semaphore()
    for d in range(1, n):
        pl.semaphore_signal(barrier, inc=1, device_id={"ctx": where[d]}, device_id_type=MESH)

    for copy in loads:
        copy.start()
    small_loads = [pltpu.make_async_copy(a, b, small_sem.at[i]) for i, (a, b) in enumerate(zip(smalls, held))]
    for copy in small_loads:
        copy.start()

    def remote(src, dst, send_sem, recv_sem, d):
        return pltpu.make_async_remote_copy(
            src_ref=src, dst_ref=dst, send_sem=send_sem, recv_sem=recv_sem,
            device_id={"ctx": where[d]}, device_id_type=MESH)

    def each(body):
        lax.fori_loop(0, blocks, lambda b, c: (body(b), c)[1], 0, unroll=True)

    def cols(b):
        return pl.ds(pl.multiple_of(b * BLOCK, BLOCK), BLOCK)

    def lanes(b, h):
        return pl.ds(pl.multiple_of(b * BLOCK + h * LANES, LANES), LANES)

    eye = (lax.broadcasted_iota(jnp.int32, (rows, rows), 0) == lax.broadcasted_iota(jnp.int32, (rows, rows), 1)).astype(BF16)

    def turn(i, b):
        x = mm_nt(eye, xin[i, cols(b), :])
        for h in range(tiles):
            xs[i, b * tiles + h, PAD:, :] = x[:, h * LANES : (h + 1) * LANES]
        tails[i, b] = pair(x[rows - 8 :, :]).astype(BF16)

    halos = [remote(tails.at[i], got_tails.at[i], tail_sem.at[0, i], tail_sem.at[1, i], 1) for i in range(3)]
    for i in range(3):
        loads[i].wait()
        each(functools.partial(turn, i))
        if i == 0:
            pl.semaphore_wait(barrier, n - 1)
        pl.when(me < n - 1)(halos[i].start)

    @pl.when(me == 0)
    def _():
        got_tails[...] = jnp.zeros_like(got_tails)

    for copy in [loads[3], *small_loads]:
        copy.wait()

    def prepare(b):
        at = cols(b)
        x = mm_nt(eye, xin[3, at, :])
        for h in range(tiles):
            cot[b * tiles + h] = x[:, h * LANES : (h + 1) * LANES]
    each(prepare)
    def gate(b, h, strips):
        t = b * tiles + h
        hl = slice(h * LANES, (h + 1) * LANES)
        skip_sum = jnp.zeros((8, LANES), F32)
        for r, size in strips:
            short = []
            for i in range(3):
                total = None
                for j in range(taps):
                    term = w_ref[i, j : j + 1, lanes(b, h)] * xs[i, t, PAD + r - j : PAD + r - j + size, :]
                    total = term if total is None else total + term
                sh[i, t, r : r + size, :] = total
                short.append(total)
            x = short[1] * short[2]
            g = cot[t, r : r + size, :] * short[0]
            gated[b, r : r + size, hl] = x.astype(BF16)
            gmix[b, r : r + size, hl] = g.astype(BF16)
            skip_sum = skip_sum + rows8(x * g)
        return skip_sum

    def inner(b):
        for h in range(tiles):
            skp[b * tiles + h] = gate(b, h, [(EDGE, STRIP - EDGE)] + [(r, STRIP) for r in range(STRIP, rows, STRIP)])

    each(inner)
    for halo in halos:
        pl.when(me < n - 1)(halo.wait_send)
        pl.when(me > 0)(halo.wait_recv)

    def edge(b):
        for i in range(3):
            halo = got_tails[i, b].astype(F32)
            for h in range(tiles):
                xs[i, b * tiles + h, :PAD, :] = halo[h * 8 : h * 8 + 8]
        for h in range(tiles):
            t = b * tiles + h
            skp[t] = skp[t] + gate(b, h, [(0, EDGE)])
        s_mom = halves(mm(back_ref[...], gated[b]))
        r_mom = halves(mm(mom_ref[...], gmix[b]))
        rmom[b] = r_mom
        for h in range(tiles):
            hl = slice(h * LANES, (h + 1) * LANES)
            wide_moms[0, :, b * tiles + h, :] = s_mom[:, hl]
            wide_moms[1, :, b * tiles + h, :] = r_mom[:, hl]

    each(edge)
    moms[...] = wide_moms[...].astype(BF16)
    states = [None] * (n - 1)
    for d in sorted(range(1, n), key=lambda d: min(d, n - d)):
        kind = jnp.where(where[d] > me, 0, 1)
        first = pl.ds(0, reach[d])
        copy = remote(moms.at[kind, first], got_moms.at[d, first], mom_send.at[d], mom_recv.at[d], d)
        copy.start()
        states[d - 1] = copy

    def filters(b):
        at = cols(b)
        dec = dec_ref[:, at]
        gain = res_ref[:, at] * jnp.sqrt(2.0 * dec)
        if few:
            carried[:, :, at] = jnp.zeros((2, modes, BLOCK), F32)
            chunk = jnp.exp(dec * (-float(rows)))
            total = jnp.ones_like(dec)
            for d in range(n - 1):
                power[d, :, at] = total
                total = total * chunk
        powers = [jnp.exp(dec * (-x)) for x in nodes]
        half = NODES // 2
        even = [powers[k] + powers[NODES - 1 - k] for k in range(half)]
        odd = [powers[k] - powers[NODES - 1 - k] for k in range(half)]
        terms = []
        for j in range(NODES):
            e = sum(turning[j][k] * (odd if j % 2 else even)[k] for k in range(half))
            e_ref[j, :, at] = e
            terms.append(gain * e)
        h_ref[b] = mm(spec_ref[...], jnp.concatenate(terms, 0).astype(BF16))

    each(filters)

    def middle(b):
        z = mm(dft_ref[...], gated[b])
        g = mm(dft_ref[...], gmix[b])
        h = h_ref[b]
        zr, zi = z[:rows], z[rows:]
        gr, gi = g[:rows], g[rows:]
        hr, hi = h[:rows], h[rows:]
        fwd = jnp.concatenate([zr * hr - zi * hi, zr * hi + zi * hr], 0).astype(BF16)
        bwd = jnp.concatenate([gr * hr + gi * hi, gi * hr - gr * hi], 0).astype(BF16)
        lag = jnp.concatenate([gr * zr + gi * zi, gi * zr - gr * zi], 0).astype(BF16)
        near[b] = mm(inv_ref[...], fwd)
        grad[b] = mm(inv_ref[...], bwd)
        moments = halves(mm(lag_ref[...], lag))
        total = jnp.zeros((modes, BLOCK), F32)
        for k in range(NODES):
            total = total + e_ref[k, :, cols(b)] * moments[k : k + 1, :]
        resp[:, cols(b)] = total

    each(middle)
    def arrived(b, d, count):
        total = None
        for j in range(count):
            x = jnp.concatenate([wide_got[d, j, pl.ds(b * tiles + h, 1), :] for h in range(tiles)], 1)
            term = e_ref[j, :, cols(b)] * x
            total = term if total is None else total + term
        return total

    def collect(d):
        states[d - 1].wait()
        wide_got[d, : reach[d]] = got_moms[d, : reach[d]].astype(F32)
        kind = jnp.where(me >= d, 0, 1)
        steps = jnp.where(me >= d, d, n - d) - 1

        def add(b):
            at = cols(b)
            carried[kind, :, at] = carried[kind, :, at] + power[steps, :, at] * arrived(b, d, reach[d])

        each(add)

    if few:
        for d in sorted(range(1, n), key=lambda d: min(d, n - d)):
            collect(d)
    else:
        for d in range(1, n):
            states[d - 1].wait()
            wide_got[d] = got_moms[d].astype(F32)

    def arrive(b):
        at = cols(b)
        dec = dec_ref[:, at]
        root = jnp.sqrt(2.0 * dec)
        one = jnp.exp(-dec)
        chunk = jnp.exp(dec * (-float(rows)))
        es = [e_ref[k, :, at] for k in range(NODES)]

        def spread(rows_of):
            total = es[0] * rows_of[0]
            for e, x in zip(es[1:], rows_of[1:]):
                total = total + e * x
            return total

        if few:
            s, r = carried[0, :, at], carried[1, :, at]
        else:
            s = r = jnp.zeros((modes, BLOCK), F32)
            s = lax.fori_loop(0, me, lambda i, s: s * chunk + arrived(b, me - i, NODES), s)
            r = lax.fori_loop(me + 1, n, lambda i, r: r * chunk + arrived(b, i, NODES), r)
        resp[:, at] = root * (resp[:, at] + one * s * spread([rmom[b, j : j + 1, :] for j in range(NODES)]))
        gain = res_ref[:, at] * root * one
        gain_s, gain_r = gain * s, gain * r
        near[b] = near[b] + mm(far_ref[...], jnp.concatenate([gain_s * e for e in es], 0).astype(BF16))
        grad[b] = grad[b] + mm(farb_ref[...], jnp.concatenate([gain_r * e for e in es], 0).astype(BF16))
        top = [[], [], []]
        for h in range(tiles):
            t = b * tiles + h
            hl = slice(h * LANES, (h + 1) * LANES)
            skip = skip_ref[:, lanes(b, h)]
            qs, ks, vs = (sh[i, t, :8, :] for i in range(3))
            c = cot[t, :8, :]
            back = grad[b, :8, hl] + skip * (c * qs)
            for i, x in enumerate((c * (near[b, :8, hl] + skip * (ks * vs)), back * vs, back * ks)):
                top[i].append(x)
        for i in range(3):
            heads[i, b] = jnp.concatenate(top[i], 0).astype(BF16)

    each(arrive)
    head = remote(heads, got_heads, head_sem.at[0], head_sem.at[1], n - 1)
    pl.when(me > 0)(head.start)

    @pl.when(me == n - 1)
    def _():
        got_heads[...] = jnp.zeros_like(got_heads)


    def last(b):
        at = cols(b)
        for h in range(tiles):
            t = b * tiles + h
            hl = slice(h * LANES, (h + 1) * LANES)
            skip = skip_ref[:, lanes(b, h)]
            sums = [jnp.zeros((8, LANES), F32)] * (3 * taps)
            for r0 in range(0, rows, STRIP):
                rr = slice(r0, r0 + STRIP)
                qs, ks, vs = (sh[i, t, rr, :] for i in range(3))
                c = cot[t, rr, :]
                mix = near[b, rr, hl] + skip * (ks * vs)
                back = grad[b, rr, hl] + skip * (c * qs)
                near[b, rr, hl] = qs * mix
                grads = (c * mix, back * vs, back * ks)
                for i in range(3):
                    gs[i, t, rr, :] = grads[i]
                    for j in range(taps):
                        shifted = xs[i, t, PAD + r0 - j : PAD + r0 - j + STRIP, :]
                        sums[i * taps + j] = sums[i * taps + j] + rows8(grads[i] * shifted)
            for a in range(3 * taps):
                acc[a * 8 : a * 8 + 8, hl] = sums[a]
            acc[3 * taps * 8 :, hl] = skp[t]
        total = jnp.concatenate([resp[:, at], mm(pick_ref[...], acc[...].astype(BF16))], 0)
        if inside:
            parted[b] = pair(total).astype(BF16)
        else:
            gres_ref[:, at] = total[:modes]
            for i in range(3):
                short_ref[i, :, at] = total[modes + 8 * i : modes + 8 * i + taps]
            gskip_ref[:, at] = total[modes + 7 : modes + 8]

    pieces = []
    if inside:
        for d in range(1, n):
            last(where[d])
            copy = remote(parted.at[where[d]], got_parts.at[d], rs_send.at[d], rs_recv.at[d], d)
            copy.start()
            pieces.append(copy)
        last(me)
    else:
        each(last)

    outs = (oq_ref, ok_ref, ov_ref)

    def final(b):
        at = cols(b)
        for i in range(3):
            halo = got_heads[i, b].astype(F32)
            for h in range(tiles):
                gs[i, b * tiles + h, rows:, :] = halo[h * 8 : h * 8 + 8]
        for h in range(tiles):
            t = b * tiles + h
            mixed_ref[lanes(b, h), :] = near[b, :, h * LANES : (h + 1) * LANES].T.astype(BF16)
            for i in range(3):
                out = []
                for r in range(0, rows, STRIP):
                    total = None
                    for j in range(taps):
                        term = w_ref[i, j : j + 1, lanes(b, h)] * gs[i, t, r + j : r + j + STRIP, :]
                        total = term if total is None else total + term
                    out.append(total)
                outs[i][lanes(b, h), :] = jnp.concatenate(out, 0).T.astype(BF16)

    if inside:
        total = parted[me].astype(F32)
        for d in range(1, n):
            pieces[d - 1].wait()
            total = total + got_parts[d].astype(F32)
        mine[...] = (total * scale).astype(BF16)
        pieces = []
        for d in range(1, n):
            copy = remote(mine, full.at[d], ag_send.at[d], ag_recv.at[d], d)
            copy.start()
            pieces.append(copy)
        full[0] = mine[...]
    pl.when(me > 0)(head.wait_send)
    pl.when(me < n - 1)(head.wait_recv)
    each(final)
    def unpack(slot, p):
        value = full[slot].astype(F32)
        for h in range(tiles):
            x, hl = value[h * height : (h + 1) * height], lanes(p, h)
            gres_ref[:, hl] = x[:modes]
            for i in range(3):
                short_ref[i, :, hl] = x[modes + 8 * i : modes + 8 * i + taps]
            gskip_ref[:, hl] = x[modes + 7 : modes + 8]

    if inside:
        height = modes + 24
        unpack(0, me)
        for d in range(1, n):
            pieces[d - 1].wait()
            unpack(d, where[n - d])


def output_kernel(*refs):
    count = (len(refs) - 1) // 2
    sems = refs[-1]
    copies = [pltpu.make_async_copy(refs[i], refs[count + i], sems.at[i]) for i in range(count)]
    for copy in copies:
        copy.start()
    for copy in copies:
        copy.wait()


def per_device(queries, key_signal, value_signal, cotangent, short_weight, residues, decay_rates, skip_gain):
    channels, rows = queries.shape
    taps = short_weight.shape[1]
    modes = residues.shape[1]
    n = lax.axis_size("ctx")
    rules, tab = tables(rows, taps, modes)
    blocks, count = channels // BLOCK, channels // LANES
    inside = channels // n == BLOCK
    scale = 1.0 / math.sqrt(rows * n)
    height = 2 * (modes + 24)
    dma = pltpu.SemaphoreType.DMA

    def shape(*dims, kind=F32):
        return jax.ShapeDtypeStruct(dims, kind)

    vmem = pl.BlockSpec(memory_space=pltpu.VMEM)
    hbm = pl.BlockSpec(memory_space=pl.ANY)
    names = ("spec", "dft", "inv", "mom", "mom_back", "lag", "far", "far_back", "pick")
    args = [decay_rates.T, residues.T, short_weight, skip_gain[None, :]] + [jnp.asarray(tab[name]) for name in names]
    owners = n if inside else 1
    mixed, gq, gk, gv, short, gres, gskip = pl.pallas_call(
        functools.partial(main_kernel, rules, taps, inside, scale),
        in_specs=[hbm] * (4 + SMALLS),
        out_specs=[vmem] * 7,
        out_shape=[pltpu.VMEM((channels, rows), BF16)] * 4 + [pltpu.VMEM((3, taps, channels), F32), pltpu.VMEM((modes, channels), F32), pltpu.VMEM((1, channels), F32)],
        scratch_shapes=[pltpu.VMEM(x.shape, x.dtype) for x in args]
        + [
            pltpu.VMEM((4, channels, rows), BF16),
            pltpu.VMEM((3, count, rows + PAD, LANES), F32),
            pltpu.VMEM((count, rows, LANES), F32),
            pltpu.VMEM((3, count, rows, LANES), F32),
            pltpu.VMEM((blocks, rows, BLOCK), BF16),
            pltpu.VMEM((blocks, rows, BLOCK), BF16),
            pltpu.VMEM((NODES, modes, channels), F32),
            pltpu.VMEM((blocks, 2 * rows, BLOCK), F32),
            pltpu.VMEM((blocks, rows, BLOCK), F32),
            pltpu.VMEM((blocks, rows, BLOCK), F32),
            pltpu.VMEM((modes, channels), F32),
            pltpu.VMEM((blocks, NODES, BLOCK), F32),
            pltpu.VMEM((count, 8, LANES), F32),
            pltpu.VMEM((3, count, rows + PAD, LANES), F32),
            pltpu.VMEM((8 * (3 * taps + 1), BLOCK), F32),
            pltpu.VMEM((3, blocks, 16, LANES), BF16),
            pltpu.VMEM((3, blocks, 16, LANES), BF16),
            pltpu.VMEM((3, blocks, 16, LANES), BF16),
            pltpu.VMEM((3, blocks, 16, LANES), BF16),
            pltpu.VMEM((2, NODES, count, LANES), BF16),
            pltpu.VMEM((n, NODES, count, LANES), BF16),
            pltpu.VMEM((2, NODES, count, LANES), F32),
            pltpu.VMEM((n, NODES, count, LANES), F32),
            pltpu.VMEM((2, modes, channels), F32),
            pltpu.VMEM((min(n, 8), modes, channels), F32),
            pltpu.VMEM((owners, height, LANES), BF16),
            pltpu.VMEM((owners, height, LANES), BF16),
            pltpu.VMEM((height, LANES), BF16),
            pltpu.VMEM((owners, height, LANES), BF16),
            dma((4,)), dma((SMALLS,)), dma((2, 3)), dma((2,)),
            dma((n,)), dma((n,)), dma((owners,)), dma((owners,)), dma((owners,)), dma((owners,)),
        ],
        compiler_params=pltpu.CompilerParams(collective_id=0, has_side_effects=True, vmem_limit_bytes=60 * 1024 * 1024),
        cost_estimate=pl.CostEstimate(flops=4 * 10**9, bytes_accessed=5 * 10**6, transcendentals=3 * 10**5),
        name="hyena",
    )(queries, key_signal, value_signal, cotangent, *args)
    if not inside:
        short, gres, gskip = (lax.psum(x, "ctx") * scale for x in (short, gres, gskip))
    else:
        values = (mixed, gq, gk, gv, short, gres, gskip)
        mixed, gq, gk, gv, short, gres, gskip = pl.pallas_call(
            output_kernel,
            in_specs=[vmem] * 7,
            out_specs=[hbm] * 7,
            out_shape=[shape(*x.shape, kind=x.dtype) for x in values],
            scratch_shapes=[dma((7,))],
            name="output",
        )(*[pltpu.with_memory_space_constraint(x, pltpu.VMEM) for x in values])
    return mixed, gq, gk, gv, short, gres.T, gskip[0]


def solution(mesh):
    signal = P("tp", "ctx")
    in_specs = (signal,) * 4 + (P(None, None, "tp"), P("tp", None), P("tp", None), P("tp"))
    out_specs = (signal,) * 4 + (P(None, None, "tp"), P("tp", None), P("tp"))
    return jax.shard_map(
        per_device, mesh=mesh, in_specs=in_specs, out_specs=out_specs, check_vma=False
    )
```
